256 devices in a mesh: group: 8 (over z), owner: 32 (over y, x, core).
Axes of the slice: x: 4, y: 4, z: 8, core: 2. Of those that a mesh axis runs over, the one named last changes fastest.
Arguments:
- port_rows: bfloat16 [131072, 1024], P(('group', 'owner')), may hold values from -6 to 6
- defect_owner: int32 [131072, 1], P(('group', 'owner')), may hold values from 0 to 31; in each aligned block of 512 rows (0 to 511, 512 to 1023, ...) at most 32 rows name the same one
- defect_half: int32 [131072], P(('group', 'owner')), may hold values from 0 to 1
- defect_port: int32 [131072], P(('group', 'owner')), may hold values from 0 to 1023
- subcircuit_maps: bfloat16 [512, 1024, 1024], P(('group', 'owner')), may hold values from -0.1875 to 0.1875
- schur_off: bfloat16 [8192, 1024], P(('group', 'owner')), may hold values from -0.1875 to 0.1875
- schur_diag: float32 [8192], P(('group', 'owner')), may hold values from 1 to 4
- pivot_order: int32 [3, 1024], replicated, may hold values from 0 to 1023, each once within a row
Outputs:
- panel: float32 [131072, 1024], P(('group', 'owner'))
The draws below stay inside these ranges and needn't reach their ends.
Inputs may be any that keep to these rules, and one draw needn't show every extreme that they name: `defect_owner`: within the rows of one device, no owner is named by more than 32 defects, a bound that some block reaches. `pivot_order`: each row is a permutation of the ports.
All inputs are finite; a program needn't handle non-finite values.
Results may differ from the reference program's by a relative error of at most 0.012.
Values may be sent and summed in bfloat16 or wider, within the bound.
No kernel may reach another device: no remote copies, remote signals or barrier semaphores. Data moves between devices by JAX's collectives and lax.ppermute only.
A program may use at most 128 MiB of HBM per device.

```python
import math
import jax
import jax.numpy as jnp
import numpy as np
from jax import lax

P_SIZE = 1024
SUB_DEV = 2
DEF_DEV = 512
LEVELS = 3
SUBS = 64
CAP = 32
DEFECTS = 131072
N_GROUP = 8
N_OWNER = 32


def place_ends(drawn, key, smallest, largest):
    index_at = [jax.random.randint(jax.random.fold_in(key, axis), (), 0, length) for axis, length in enumerate(drawn.shape)]
    longest = drawn.shape.index(max(drawn.shape))
    neighbour = index_at[:longest] + [(index_at[longest] + 1) % drawn.shape[longest]] + index_at[longest + 1:]
    return drawn.at[tuple(index_at)].set(smallest).at[tuple(neighbour)].set(largest)


def block_scale(own_key, dims, shards, smallest, high):
    def one(axis_at, shards_of):
        draws = jax.random.uniform(jax.random.fold_in(jax.random.fold_in(own_key, 6), axis_at), (shards_of,), jnp.float32, smallest / len(shards), high / len(shards))
        return jnp.repeat(jnp.exp(draws), dims[axis_at] // shards_of).reshape((-1,) + (1,) * (len(dims) - axis_at - 1))

    factor_of = one(*shards[0])
    for cut in shards[1:]:
        factor_of = factor_of * one(*cut)
    return factor_of


def deal_out(stream_key, own, number, rows, count, top, most, slope):
    ranking = jax.random.permutation(stream_key, count)
    heavy_load, common = load_shares(count, rows * top, most, slope, True), load_shares(count, rows * top, most, slope, False)
    places = jnp.arange(count)

    def named(sizes, turn):
        used = int((sizes > 0).sum())
        fixed = max(1, used // 4)
        passed = fixed + (places - fixed + turn * (used - fixed)) % max(1, count - fixed)
        return jnp.zeros((count,), jnp.int32).at[ranking[jnp.where(places < fixed, places, passed)]].set(jnp.asarray(sizes, jnp.int32))

    sizes = jnp.where(number % 4 == 0, named(heavy_load, number // 4), named(common, number - number // 4 - 1))
    mixed = jax.random.permutation(jax.random.fold_in(own, 3), count)
    donor, taker = mixed[0:count // 2 * 2:2], mixed[1:count // 2 * 2:2]
    room = jnp.minimum(sizes[donor] - 1, most - sizes[taker]) // 2
    room = jnp.where((donor == ranking[0]) | (taker == ranking[0]) | (sizes[taker] == 0), 0, jnp.maximum(room, 0))
    passed = jax.random.randint(jax.random.fold_in(own, 4), (count // 2,), 0, 1 << 20) % (room + 1)
    sizes = sizes.at[donor].add(-passed).at[taker].add(passed)
    labels = jnp.searchsorted(jnp.cumsum(sizes), jnp.arange(rows * top), side="right").astype(jnp.int32)
    grid = labels.reshape(top, rows).T
    grid = grid[jax.random.permutation(jax.random.fold_in(own, 1), rows)]
    turn = jax.random.randint(jax.random.fold_in(own, 2), (rows, 1), 0, top)
    return jnp.take_along_axis(grid, (jnp.arange(top)[None, :] + turn) % top, axis=1)


def load_shares(count, total, most, slope, full):
    portions = [(1 << 20) // math.isqrt(rank ** slope) + 1 for rank in range(1, count + 1)]
    largest = most if full else min(most, max(-(-total // count), total * portions[0] // sum(portions)))
    least = 1 if total - largest >= count - 1 else 0
    holding, spare = [largest] + [least] * (count - 1), total - largest - least * (count - 1)
    while spare > 0:
        movable = [i for i in range(1, count) if holding[i] < largest] or [i for i in range(1, count) if holding[i] < most]
        pool, remaining = sum([portions[i] for i in movable]), spare
        for i in movable:
            extra = min(most - holding[i], max(1, remaining * portions[i] // pool), spare)
            holding[i] = holding[i] + extra
            spare = spare - extra
    return np.array(holding)


def noise(own_key, extent, width, reach, shards=(), held_as=jnp.bfloat16):
    values = jax.random.normal(own_key, extent, jnp.float32) * width
    if len(shards) > 0:
        values = block_scale(own_key, extent, shards, -0.22, 0.18) * values
    return jnp.clip(values, min=-reach, max=reach).astype(held_as)


def setup_inputs(seed: int = 0) -> dict:
    key_list = jax.random.split(jax.random.key(seed), 9)
    port_rows = noise(key_list[0], (DEFECTS, P_SIZE), 1.0, 6.0, ((0, 256),))
    defect_owner_keys = jax.random.split(jax.random.fold_in(key_list[1], 1), DEFECTS // DEF_DEV)
    defect_owner_turns = jax.random.permutation(jax.random.fold_in(key_list[1], 3), DEFECTS // DEF_DEV)
    defect_owner = jax.vmap(lambda own, number: deal_out(jax.random.fold_in(key_list[1], 2), own, number, DEF_DEV, N_OWNER, 1, CAP, 2))(defect_owner_keys, defect_owner_turns).reshape((DEFECTS, 1))
    defect_half = place_ends(jax.random.randint(key_list[2], (DEFECTS,), 0, SUB_DEV), jax.random.fold_in(key_list[2], 1), 0, SUB_DEV - 1).astype(jnp.int32)
    defect_port = place_ends(jax.random.randint(key_list[3], (DEFECTS,), 0, P_SIZE), jax.random.fold_in(key_list[3], 1), 0, P_SIZE - 1).astype(jnp.int32)
    subcircuit_maps = noise(key_list[4], (N_GROUP * SUBS, P_SIZE, P_SIZE), P_SIZE ** -0.5, 0.1875, ((0, 256),))
    schur_off = noise(key_list[5], (N_GROUP * P_SIZE, P_SIZE), P_SIZE ** -0.5, 0.1875, ((0, 256),))
    schur_diag = jnp.clip(jnp.exp(math.log(4.0) - 1.3862944 * jax.random.uniform(key_list[6], (N_GROUP * P_SIZE,), jnp.float32) ** block_scale(key_list[6], (N_GROUP * P_SIZE,), ((0, 256),), -0.2, 0.2)), 1.0, 4.0)
    pivot_order = jax.vmap(lambda own: jax.random.permutation(own, P_SIZE))(jax.random.split(key_list[7], LEVELS)).reshape((LEVELS, P_SIZE)).astype(jnp.int32)
    return dict(port_rows=port_rows, defect_owner=defect_owner, defect_half=defect_half, defect_port=defect_port, subcircuit_maps=subcircuit_maps, schur_off=schur_off, schur_diag=schur_diag, pivot_order=pivot_order)


def one_group(pieces):
    stim_group, sub_group, maps_group = pieces
    all_subs = SUB_DEV * N_OWNER
    matches = (sub_group[:, :, None] == jnp.arange(all_subs, dtype=jnp.int32)[None, None, :]).astype(jnp.int32)
    before = jnp.cumsum(matches, axis=1) - matches
    slot_rank = jnp.sum(before * matches, axis=2)
    target = sub_group * CAP + slot_rank
    route_table = (lax.broadcasted_iota(jnp.int32, (N_OWNER, all_subs * CAP, DEF_DEV), 1) == target[:, None, :]).astype(jnp.float32)
    buffers = jnp.einsum("oud,odp->oup", route_table, stim_group.astype(jnp.float32))
    buffers = buffers.reshape(N_OWNER, all_subs, CAP, P_SIZE)
    answers = jnp.einsum("oscp,spq->oscq", buffers, maps_group.astype(jnp.float32)).astype(jnp.bfloat16)
    answers = lax.optimization_barrier(answers)
    flat_answers = answers.reshape(N_OWNER, all_subs * CAP, P_SIZE).astype(jnp.float32)
    return jnp.einsum("oud,oup->odp", route_table, flat_answers)


def couple_group(pieces):
    panel_group, block_group = pieces
    return lax.dot_general(panel_group.astype(jnp.bfloat16), block_group.astype(jnp.bfloat16), (((1,), (1,)), ((), ())), preferred_element_type=jnp.float32)


def reference(port_rows, defect_owner, defect_half, defect_port, subcircuit_maps, schur_off, schur_diag, pivot_order):
    all_subs = SUB_DEV * N_OWNER
    columns = lax.broadcasted_iota(jnp.int32, (DEFECTS, P_SIZE), 1)
    stimulus = (port_rows.astype(jnp.float32) + jnp.where(columns == defect_port[:, None], 8.0, 0.0)).astype(jnp.bfloat16)
    sub_ids = (defect_owner[:, 0] * SUB_DEV + defect_half).astype(jnp.int32)
    stim_groups = stimulus.reshape(N_GROUP, N_OWNER, DEF_DEV, P_SIZE)
    sub_groups = sub_ids.reshape(N_GROUP, N_OWNER, DEF_DEV)
    map_groups = subcircuit_maps.reshape(N_GROUP, all_subs, P_SIZE, P_SIZE)
    responses = lax.map(one_group, (stim_groups, sub_groups, map_groups))
    response = responses.reshape(N_GROUP, N_OWNER * DEF_DEV, P_SIZE)
    blocks = schur_off.reshape(N_GROUP, P_SIZE, P_SIZE).astype(jnp.float32)
    diags = schur_diag.reshape(N_GROUP, P_SIZE)
    panel = response / diags[:, None, :]
    indices = np.arange(N_GROUP)
    for level in range(LEVELS):
        partner = indices ^ (1 << level)
        blocks = blocks + jnp.take(blocks[partner], pivot_order[level], axis=2)
        diags = diags + diags[partner]
        coupled = lax.map(couple_group, (panel, blocks))
        panel = (response - coupled) / diags[:, None, :]
    return panel.reshape(DEFECTS, P_SIZE)
```

```python
import jax
import jax.numpy as jnp
from jax import lax
from jax.experimental import pallas as pl
from jax.experimental.pallas import tpu as pltpu
from jax.sharding import PartitionSpec as P

BF16 = jnp.bfloat16
F32 = jnp.float32
I32 = jnp.int32

ROWS = 512
PORTS = 1024
OWNERS = 32
CAP = 32
SLOTS = OWNERS * CAP
OWN = 32
DROWS = 8
ZROWS = OWN + DROWS
PACK = 3 * OWN + DROWS
HALF_SCALE = 64.0
HALF_MARK = 32.0
STEPS = (1, -1, 2)
NEAR = (0, -1, 1, -2)


def iota(shape, dim):
    return lax.broadcasted_iota(I32, shape, dim)


def params(limit=48, dims=None):
    return pltpu.CompilerParams(vmem_limit_bytes=limit << 20, dimension_semantics=dims)


def cost(flops, nbytes):
    return pl.CostEstimate(flops=flops, bytes_accessed=nbytes, transcendentals=0)


def split(value, parts):
    pieces = []
    for _ in range(parts):
        piece = value.astype(BF16).astype(F32)
        pieces.append(piece)
        value = value - piece
    return pieces


def rows_of(pieces, count):
    r = iota((count, PORTS), 0)
    out = jnp.zeros((count, PORTS), F32)
    for k, piece in enumerate(pieces):
        out = jnp.where(r == k, piece, out)
    return out.astype(BF16)


def own_lanes():
    own = lax.axis_index("owner")
    return iota((OWN, PORTS), 1) == own * OWN + iota((OWN, PORTS), 0)


def prep_kernel(owner_ref, half_ref, port_ref, rows_ref, off_ref, diag_ref, out_ref, target_ref, z_ref, stim):
    step = pl.program_id(0)
    tile = out_ref.shape[0]

    @pl.when(step == 0)
    def _():
        owner = owner_ref[...]
        named = iota((OWNERS, ROWS), 0) == owner
        earlier = jnp.where(iota((ROWS, ROWS), 0) < iota((ROWS, ROWS), 1), 1.0, 0.0).astype(BF16)
        before = jnp.dot(jnp.where(named, 1.0, 0.0).astype(BF16), earlier, preferred_element_type=F32)
        rank = jnp.sum(jnp.where(named, before, 0.0), axis=0, keepdims=True)
        target_ref[...] = owner * CAP + rank.astype(I32)
        port = jnp.transpose(jnp.broadcast_to(port_ref[...], (128, ROWS)))
        for j in range(PORTS // 128):
            lanes = slice(128 * j, 128 * j + 128)
            bump = jnp.where(iota((ROWS, 128), 1) + 128 * j == port, 8.0, 0.0)
            stim[:, lanes] = (rows_ref[:, lanes].astype(F32) + bump).astype(BF16)
        z_ref[:OWN, :] = off_ref[...]
        diag = jnp.sum(
            jnp.where(iota((OWN, OWN), 0) == iota((OWN, OWN), 1), diag_ref[...], 0.0), axis=1, keepdims=True
        )
        placed = jnp.sum(jnp.where(own_lanes(), diag, 0.0), axis=0, keepdims=True)
        z_ref[OWN:, :] = rows_of(split(placed, 3), DROWS)

    scale = jnp.where(half_ref[...] == 1, HALF_SCALE, 1.0)
    route = jnp.where(iota((tile, ROWS), 0) + step * tile == target_ref[...], scale, 0.0).astype(BF16)
    out_ref[...] = jnp.dot(route, stim[...], preferred_element_type=F32).astype(BF16)


def prep(owner, half, port, rows, off, diag):
    tile = 256
    whole = lambda *shape: pl.BlockSpec(shape, lambda i: (0,) * len(shape))
    return pl.pallas_call(
        prep_kernel,
        grid=(SLOTS // tile,),
        in_specs=[
            whole(1, ROWS), whole(1, ROWS), whole(1, ROWS), whole(ROWS, PORTS), whole(OWN, PORTS), whole(1, OWN),
        ],
        out_specs=[pl.BlockSpec((tile, PORTS), lambda i: (i, 0)), whole(1, ROWS), whole(ZROWS, PORTS)],
        out_shape=[
            jax.ShapeDtypeStruct((SLOTS, PORTS), BF16),
            jax.ShapeDtypeStruct((1, ROWS), I32),
            jax.ShapeDtypeStruct((ZROWS, PORTS), BF16),
        ],
        scratch_shapes=[pltpu.VMEM((ROWS, PORTS), BF16)],
        compiler_params=params(),
        cost_estimate=cost(2 * SLOTS * ROWS * PORTS, 4 << 20),
        name="prep",
    )(owner, half, port, rows, off, diag)


def maps_kernel(x_ref, maps_ref, out_ref):
    x = x_ref[...]
    second = jnp.max(jnp.abs(x.astype(F32)), axis=1, keepdims=True) > HALF_MARK
    first_rows = jnp.where(second, 0.0, x.astype(F32)).astype(BF16)
    second_rows = jnp.where(second, x.astype(F32) * (1.0 / HALF_SCALE), 0.0).astype(BF16)
    acc = jnp.dot(first_rows, maps_ref[0], preferred_element_type=F32)
    acc = acc + jnp.dot(second_rows, maps_ref[1], preferred_element_type=F32)
    out_ref[...] = acc.astype(BF16)


def apply_maps(x, maps):
    tile = 256
    return pl.pallas_call(
        maps_kernel,
        grid=(SLOTS // tile,),
        in_specs=[
            pl.BlockSpec((tile, PORTS), lambda i: (i, 0)),
            pl.BlockSpec((2, PORTS, PORTS), lambda i: (0, 0, 0)),
        ],
        out_specs=pl.BlockSpec((tile, PORTS), lambda i: (i, 0)),
        out_shape=jax.ShapeDtypeStruct((SLOTS, PORTS), BF16),
        compiler_params=params(),
        cost_estimate=cost(4 * SLOTS * PORTS * PORTS, 8 << 20),
        name="apply_maps",
    )(x, maps)


def permuted(values, order):
    out = jnp.zeros(values.shape, F32)
    for j in range(0, PORTS, 256):
        pick = jnp.where(iota((256, PORTS), 0) + j == order, 1.0, 0.0).astype(BF16)
        out = out + jnp.dot(values[:, j : j + 256], pick, preferred_element_type=F32)
    return out


def read_diag(z_ref):
    z = z_ref[OWN:, :].astype(F32)
    return z[0:1] + z[1:2] + z[2:3]


def column(placed):
    return jnp.sum(jnp.where(own_lanes(), placed, 0.0), axis=1, keepdims=True)


def inverse(placed):
    held = placed > 0.0
    return jnp.where(held, 1.0 / jnp.where(held, placed, 1.0), 0.0)


def low_levels_kernel(z0_ref, z1_ref, z2_ref, z3_ref, order_ref, z_ref, off_ref, diag_ref, gb_ref):
    picked = permuted(jnp.concatenate([z1_ref[:OWN, :], z3_ref[:OWN, :]], axis=0), order_ref[0:1, :])
    off1 = z0_ref[:OWN, :].astype(F32) + picked[:OWN]
    picked2 = permuted(jnp.concatenate([z2_ref[:OWN, :], picked[OWN:].astype(BF16)], axis=0), order_ref[1:2, :])
    off2 = off1 + (picked2[:OWN] + picked2[OWN:])
    d0 = read_diag(z0_ref)
    d1 = d0 + read_diag(z1_ref)
    d2 = d1 + (read_diag(z2_ref) + read_diag(z3_ref))
    z_ref[:OWN, :] = off2.astype(BF16)
    z_ref[OWN:, :] = rows_of(split(d2, 3), DROWS)
    off_ref[...] = off2
    r = iota((DROWS, PORTS), 0)
    diag_ref[...] = jnp.where(r == 0, d0, jnp.where(r == 1, d2, 0.0))
    gb_ref[:OWN, :] = ((jnp.where(own_lanes(), d0, 0.0) - off1) / column(d1)).astype(BF16)
    gb_ref[OWN:, :] = (off2 / column(d2)).astype(BF16)


def low_levels(z0, z1, z2, z3, order):
    return pl.pallas_call(
        low_levels_kernel,
        out_shape=[
            jax.ShapeDtypeStruct((ZROWS, PORTS), BF16),
            jax.ShapeDtypeStruct((OWN, PORTS), F32),
            jax.ShapeDtypeStruct((DROWS, PORTS), F32),
            jax.ShapeDtypeStruct((2 * OWN, PORTS), BF16),
        ],
        compiler_params=params(),
        cost_estimate=cost(4 * 64 * PORTS * PORTS, 1 << 20),
        name="low_levels",
    )(z0, z1, z2, z3, order)


def top_level_kernel(z4_ref, off_ref, diag_ref, gb_ref, order_ref, pack_ref):
    off3 = off_ref[...] + permuted(z4_ref[:OWN, :], order_ref[2:3, :])
    d0, d2 = diag_ref[0:1, :], diag_ref[1:2, :]
    d3 = d2 + read_diag(z4_ref)
    pack_ref[: 2 * OWN, :] = gb_ref[...]
    pack_ref[2 * OWN : 3 * OWN, :] = (off3 / column(d3)).astype(BF16)
    pieces = split(inverse(d0), 3) + split(inverse(d3), 3) + split(d0 * inverse(d2), 2)
    pack_ref[3 * OWN :, :] = rows_of(pieces, DROWS)


def top_level(z4, off, diag, gb, order):
    return pl.pallas_call(
        top_level_kernel,
        out_shape=jax.ShapeDtypeStruct((PACK, PORTS), BF16),
        compiler_params=params(),
        cost_estimate=cost(2 * 32 * PORTS * PORTS, 1 << 20),
        name="top_level",
    )(z4, off, diag, gb, order)


def fold_kernel(*refs):
    parts, (f_ref, diag_ref, held, marks, mid, sems) = refs[:8], refs[8:]
    own = lax.axis_index("owner")
    core, x, y = own & 1, (own >> 1) & 3, own >> 3
    copies = []
    slot = 0
    for side in range(2):
        c = core if side == 0 else 1 - core
        for m in range(4):
            for k in range(4):
                dx = jnp.where(c == 0, NEAR[k], NEAR[m])
                dy = jnp.where(c == 0, NEAR[m], NEAR[k])
                start = ((((y + dy) & 3) * 4 + ((x + dx) & 3)) * 2 + c) * OWN
                start = pl.multiple_of(start, OWN)
                block = parts[side * 4 + m].at[k]
                for j in range(3):
                    copies.append(
                        pltpu.make_async_copy(
                            block.at[pl.ds(j * OWN, OWN), :], held.at[j, pl.ds(start, OWN), :], sems.at[j]
                        )
                    )
                copies.append(pltpu.make_async_copy(block.at[pl.ds(3 * OWN, DROWS), :], marks.at[slot], sems.at[3]))
                slot += 1
    for copy in copies:
        copy.start()
    for copy in copies:
        copy.wait()
    total = jnp.sum(marks[...].astype(F32), axis=0)
    inv0 = total[0:1] + total[1:2] + total[2:3]
    inv3 = total[3:4] + total[4:5] + total[5:6]
    ratio = total[6:7] + total[7:8]
    r = iota((DROWS, PORTS), 0)
    diag_ref[...] = jnp.where(r == 0, inv0, jnp.where(r == 1, inv3, 0.0))
    tile = 256

    @pl.loop(0, PORTS // tile)
    def _(t):
        at = pl.ds(pl.multiple_of(t * tile, tile), tile)
        acc = jnp.dot(held[1, at, :], held[0], preferred_element_type=F32)
        on = iota((tile, PORTS), 1) == iota((tile, PORTS), 0) + t * tile
        mid[at, :] = (jnp.where(on, ratio, 0.0) - acc).astype(BF16)

    @pl.loop(0, PORTS // tile)
    def _(t):
        at = pl.ds(pl.multiple_of(t * tile, tile), tile)
        f_ref[at, :] = jnp.dot(held[2, at, :], mid[...], preferred_element_type=F32).astype(BF16)


def fold(parts):
    return pl.pallas_call(
        fold_kernel,
        in_specs=[pl.BlockSpec(memory_space=pl.ANY)] * 8,
        out_shape=[jax.ShapeDtypeStruct((PORTS, PORTS), BF16), jax.ShapeDtypeStruct((DROWS, PORTS), F32)],
        scratch_shapes=[
            pltpu.VMEM((3, PORTS, PORTS), BF16),
            pltpu.VMEM((32, DROWS, PORTS), BF16),
            pltpu.VMEM((PORTS, PORTS), BF16),
            pltpu.SemaphoreType.DMA((4,)),
        ],
        compiler_params=params(),
        cost_estimate=cost(4 * PORTS**3, 9 << 20),
        name="fold",
    )(*parts)


def finish_kernel(target_ref, ret_ref, f_ref, diag_ref, out_ref):
    tile = out_ref.shape[0]
    target = jnp.transpose(jnp.broadcast_to(target_ref[...], (128, tile)))
    route = jnp.concatenate(
        [
            jnp.where(iota((tile, 128), 1) + 128 * j == target, 1.0, 0.0).astype(BF16)
            for j in range(SLOTS // 128)
        ],
        axis=1,
    )
    response = jnp.dot(route, ret_ref[...], preferred_element_type=F32)
    scaled = (response * diag_ref[0:1, :]).astype(BF16)
    coupled = lax.dot_general(scaled, f_ref[...], (((1,), (1,)), ((), ())), preferred_element_type=F32)
    out_ref[...] = response * diag_ref[1:2, :] - coupled


def finish(target, returned, f, diag):
    tile = 128
    whole = lambda *shape: pl.BlockSpec(shape, lambda i: (0,) * len(shape))
    return pl.pallas_call(
        finish_kernel,
        grid=(ROWS // tile,),
        in_specs=[
            pl.BlockSpec((1, tile), lambda i: (0, i)), whole(SLOTS, PORTS), whole(PORTS, PORTS), whole(DROWS, PORTS),
        ],
        out_specs=pl.BlockSpec((tile, PORTS), lambda i: (i, 0)),
        out_shape=jax.ShapeDtypeStruct((ROWS, PORTS), F32),
        compiler_params=params(),
        cost_estimate=cost(4 * ROWS * PORTS * PORTS, 6 << 20),
        name="finish",
    )(target, returned, f, diag)


def group_swap(value, mask):
    return lax.ppermute(value, "group", [(i, i ^ mask) for i in range(8)])


def chip_shift(value, step, turn):
    pairs = []
    for o in range(OWNERS):
        c, x, y = o & 1, (o >> 1) & 3, o >> 3
        if (c ^ turn) == 0:
            x = (x + step) % 4
        else:
            y = (y + step) % 4
        pairs.append((o, (y * 4 + x) * 2 + c))
    return lax.ppermute(value, "owner", pairs)


def core_swap(value):
    return lax.ppermute(value, "owner", [(o, o ^ 1) for o in range(OWNERS)])


def exchange(value):
    shape = value.shape
    value = value.reshape(OWNERS, CAP, PORTS)
    return lax.all_to_all(value, "owner", split_axis=0, concat_axis=0, tiled=True).reshape(shape)


def body(port_rows, defect_owner, defect_half, defect_port, subcircuit_maps, schur_off, schur_diag, pivot_order):
    outgoing, target, z0 = prep(
        defect_owner.reshape(1, ROWS),
        defect_half.reshape(1, ROWS),
        defect_port.reshape(1, ROWS),
        port_rows,
        schur_off,
        schur_diag.reshape(1, OWN),
    )
    arrived = exchange(outgoing)
    z1, z2, z3 = (group_swap(z0, mask) for mask in (1, 2, 3))
    z, off, diag, gb = low_levels(z0, z1, z2, z3, pivot_order)
    pack = top_level(group_swap(z, 4), off, diag, gb, pivot_order)
    line = jnp.stack([pack] + [chip_shift(pack, step, 0) for step in STEPS])
    parts = [line] + [chip_shift(line, step, 1) for step in STEPS]
    parts = parts + [core_swap(part) for part in parts]
    f, inverses = fold(parts)
    answers = apply_maps(arrived, subcircuit_maps)
    returned = exchange(answers)
    return finish(target, returned, f, inverses)


def solution(mesh):
    return jax.shard_map(
        body,
        mesh=mesh,
        in_specs=(
            P(("group", "owner"), None),
            P(("group", "owner"), None),
            P(("group", "owner")),
            P(("group", "owner")),
            P(("group", "owner"), None, None),
            P(("group", "owner"), None),
            P(("group", "owner")),
            P(),
        ),
        out_specs=P(("group", "owner"), None),
        check_vma=False,
    )
```

```python
import jax
import jax.numpy as jnp
from jax import lax
from jax.experimental import pallas as pl
from jax.experimental.pallas import tpu as pltpu
from jax.sharding import PartitionSpec as P

BF16 = jnp.bfloat16
F32 = jnp.float32
I32 = jnp.int32

ROWS = 512
PORTS = 1024
OWNERS = 32
CAP = 32
SLOTS = OWNERS * CAP
OWN = 32
DROWS = 8
ZROWS = OWN + DROWS
PACK = 3 * OWN + DROWS
HALF_SCALE = 64.0
HALF_MARK = 32.0
STEPS = (1, -1, 2)
NEAR = (0, -1, 1, -2)


def iota(shape, dim):
    return lax.broadcasted_iota(I32, shape, dim)


def params(limit=48, dims=None):
    return pltpu.CompilerParams(vmem_limit_bytes=limit << 20, dimension_semantics=dims)


def cost(flops, nbytes):
    return pl.CostEstimate(flops=flops, bytes_accessed=nbytes, transcendentals=0)


def hbm(value):
    return pltpu.with_memory_space_constraint(value, pltpu.HBM)


def whole(*shape):
    return pl.BlockSpec(shape, lambda i: (0,) * len(shape))


def split(value, parts):
    pieces = []
    for _ in range(parts):
        piece = value.astype(BF16).astype(F32)
        pieces.append(piece)
        value = value - piece
    return pieces


def rows_of(pieces, count):
    r = iota((count, PORTS), 0)
    out = jnp.zeros((count, PORTS), F32)
    for k, piece in enumerate(pieces):
        out = jnp.where(r == k, piece, out)
    return out.astype(BF16)


def own_lanes():
    own = lax.axis_index("owner")
    return iota((OWN, PORTS), 1) == own * OWN + iota((OWN, PORTS), 0)


def label_kernel(off_ref, diag_ref, z_ref):
    z_ref[:OWN, :] = off_ref[...]
    diag = jnp.sum(jnp.where(iota((OWN, OWN), 0) == iota((OWN, OWN), 1), diag_ref[...], 0.0), axis=1, keepdims=True)
    placed = jnp.sum(jnp.where(own_lanes(), diag, 0.0), axis=0, keepdims=True)
    z_ref[OWN:, :] = rows_of(split(placed, 3), DROWS)


def label(off, diag):
    return pl.pallas_call(
        label_kernel,
        out_shape=jax.ShapeDtypeStruct((ZROWS, PORTS), BF16),
        compiler_params=params(),
        cost_estimate=cost(OWN * PORTS, 1 << 17),
        name="label",
    )(hbm(off), hbm(diag))


def prep_kernel(owner_ref, half_ref, port_ref, rows_ref, z_ref, out_ref, target_ref, stim):
    step = pl.program_id(0)
    tile = out_ref.shape[0]

    @pl.when(step == 0)
    def _():
        owner = owner_ref[...]
        named = iota((OWNERS, ROWS), 0) == owner
        earlier = jnp.where(iota((ROWS, ROWS), 0) < iota((ROWS, ROWS), 1), 1.0, 0.0).astype(BF16)
        before = jnp.dot(jnp.where(named, 1.0, 0.0).astype(BF16), earlier, preferred_element_type=F32)
        rank = jnp.sum(jnp.where(named, before, 0.0), axis=0, keepdims=True)
        target_ref[...] = owner * CAP + rank.astype(I32)
        port = jnp.transpose(jnp.broadcast_to(port_ref[...], (128, ROWS)))
        for j in range(PORTS // 128):
            lanes = slice(128 * j, 128 * j + 128)
            bump = jnp.where(iota((ROWS, 128), 1) + 128 * j == port, 8.0, 0.0)
            stim[:, lanes] = (rows_ref[:, lanes].astype(F32) + bump).astype(BF16)

    scale = jnp.where(half_ref[...] == 1, HALF_SCALE, 1.0)
    route = jnp.where(iota((tile, ROWS), 0) + step * tile == target_ref[...], scale, 0.0).astype(BF16)
    out_ref[...] = jnp.dot(route, stim[...], preferred_element_type=F32).astype(BF16)


def prep(owner, half, port, rows, z):
    tile = 256
    return pl.pallas_call(
        prep_kernel,
        grid=(SLOTS // tile,),
        in_specs=[
            whole(1, ROWS), whole(1, ROWS), whole(1, ROWS), whole(ROWS, PORTS), pl.BlockSpec(memory_space=pl.ANY),
        ],
        out_specs=[pl.BlockSpec((tile, PORTS), lambda i: (i, 0)), whole(1, ROWS)],
        out_shape=[pltpu.HBM((SLOTS, PORTS), BF16), jax.ShapeDtypeStruct((1, ROWS), I32)],
        scratch_shapes=[pltpu.VMEM((ROWS, PORTS), BF16)],
        compiler_params=params(),
        cost_estimate=cost(2 * SLOTS * ROWS * PORTS, 4 << 20),
        name="prep",
    )(hbm(owner), hbm(half), hbm(port), hbm(rows), z)


def maps_kernel(x_ref, maps_ref, out_ref, first, other):
    @pl.when(pl.program_id(0) == 0)
    def _():
        for r in range(0, SLOTS, 256):
            x = x_ref[r : r + 256, :].astype(F32)
            second = jnp.max(jnp.abs(x), axis=1, keepdims=True) > HALF_MARK
            first[r : r + 256, :] = jnp.where(second, 0.0, x).astype(BF16)
            other[r : r + 256, :] = jnp.where(second, x * (1.0 / HALF_SCALE), 0.0).astype(BF16)

    acc = jnp.dot(first[...], maps_ref[0], preferred_element_type=F32)
    acc = acc + jnp.dot(other[...], maps_ref[1], preferred_element_type=F32)
    out_ref[...] = acc.astype(BF16)


def apply_maps(x, maps):
    tile = 256
    return pl.pallas_call(
        maps_kernel,
        grid=(PORTS // tile,),
        in_specs=[whole(SLOTS, PORTS), pl.BlockSpec((2, PORTS, tile), lambda i: (0, 0, i))],
        out_specs=pl.BlockSpec((SLOTS, tile), lambda i: (0, i)),
        out_shape=pltpu.HBM((SLOTS, PORTS), BF16),
        scratch_shapes=[pltpu.VMEM((SLOTS, PORTS), BF16), pltpu.VMEM((SLOTS, PORTS), BF16)],
        compiler_params=params(),
        cost_estimate=cost(4 * SLOTS * PORTS * PORTS, 8 << 20),
        name="apply_maps",
    )(x, hbm(maps))


def permuted(values, order):
    out = jnp.zeros(values.shape, F32)
    for j in range(0, PORTS, 256):
        pick = jnp.where(iota((256, PORTS), 0) + j == order, 1.0, 0.0).astype(BF16)
        out = out + jnp.dot(values[:, j : j + 256], pick, preferred_element_type=F32)
    return out


def read_diag(z_ref):
    z = z_ref[OWN:, :].astype(F32)
    return z[0:1] + z[1:2] + z[2:3]


def column(placed):
    return jnp.sum(jnp.where(own_lanes(), placed, 0.0), axis=1, keepdims=True)


def inverse(placed):
    held = placed > 0.0
    return jnp.where(held, 1.0 / jnp.where(held, placed, 1.0), 0.0)


def low_levels_kernel(z0_ref, z1_ref, z2_ref, z3_ref, order_ref, z_ref, off_ref, diag_ref, gb_ref):
    picked = permuted(jnp.concatenate([z1_ref[:OWN, :], z3_ref[:OWN, :]], axis=0), order_ref[0:1, :])
    off1 = z0_ref[:OWN, :].astype(F32) + picked[:OWN]
    picked2 = permuted(jnp.concatenate([z2_ref[:OWN, :], picked[OWN:].astype(BF16)], axis=0), order_ref[1:2, :])
    off2 = off1 + (picked2[:OWN] + picked2[OWN:])
    d0 = read_diag(z0_ref)
    d1 = d0 + read_diag(z1_ref)
    d2 = d1 + (read_diag(z2_ref) + read_diag(z3_ref))
    z_ref[:OWN, :] = off2.astype(BF16)
    z_ref[OWN:, :] = rows_of(split(d2, 3), DROWS)
    off_ref[...] = off2
    r = iota((DROWS, PORTS), 0)
    diag_ref[...] = jnp.where(r == 0, d0, jnp.where(r == 1, d2, 0.0))
    gb_ref[:OWN, :] = ((jnp.where(own_lanes(), d0, 0.0) - off1) / column(d1)).astype(BF16)
    gb_ref[OWN:, :] = (off2 / column(d2)).astype(BF16)


def low_levels(z0, z1, z2, z3, order):
    return pl.pallas_call(
        low_levels_kernel,
        out_shape=[
            jax.ShapeDtypeStruct((ZROWS, PORTS), BF16),
            jax.ShapeDtypeStruct((OWN, PORTS), F32),
            jax.ShapeDtypeStruct((DROWS, PORTS), F32),
            jax.ShapeDtypeStruct((2 * OWN, PORTS), BF16),
        ],
        compiler_params=params(),
        cost_estimate=cost(4 * 64 * PORTS * PORTS, 1 << 20),
        name="low_levels",
    )(z0, z1, z2, z3, order)


def top_level_kernel(z4_ref, off_ref, diag_ref, gb_ref, order_ref, pack_ref):
    off3 = off_ref[...] + permuted(z4_ref[:OWN, :], order_ref[2:3, :])
    d0, d2 = diag_ref[0:1, :], diag_ref[1:2, :]
    d3 = d2 + read_diag(z4_ref)
    pack_ref[: 2 * OWN, :] = gb_ref[...]
    pack_ref[2 * OWN : 3 * OWN, :] = (off3 / column(d3)).astype(BF16)
    pieces = split(inverse(d0), 3) + split(inverse(d3), 3) + split(d0 * inverse(d2), 2)
    pack_ref[3 * OWN :, :] = rows_of(pieces, DROWS)


def top_level(z4, off, diag, gb, order):
    return pl.pallas_call(
        top_level_kernel,
        out_shape=jax.ShapeDtypeStruct((PACK, PORTS), BF16),
        compiler_params=params(),
        cost_estimate=cost(2 * 32 * PORTS * PORTS, 1 << 20),
        name="top_level",
    )(z4, off, diag, gb, order)


def fold_kernel(*refs):
    parts, (f_ref, diag_ref, held, marks, sems) = refs[:8], refs[8:]
    own = lax.axis_index("owner")
    core, x, y = own & 1, (own >> 1) & 3, own >> 3
    copies = []
    slot = 0
    for side in range(2):
        c = core if side == 0 else 1 - core
        for m in range(4):
            for k in range(4):
                dx = jnp.where(c == 0, NEAR[k], NEAR[m])
                dy = jnp.where(c == 0, NEAR[m], NEAR[k])
                start = ((((y + dy) & 3) * 4 + ((x + dx) & 3)) * 2 + c) * OWN
                start = pl.multiple_of(start, OWN)
                block = parts[side * 4 + m].at[k]
                for j in range(3):
                    copies.append(
                        pltpu.make_async_copy(
                            block.at[pl.ds(j * OWN, OWN), :], held.at[j, pl.ds(start, OWN), :], sems.at[j]
                        )
                    )
                copies.append(pltpu.make_async_copy(block.at[pl.ds(3 * OWN, DROWS), :], marks.at[slot], sems.at[3]))
                slot += 1
    for copy in copies:
        copy.start()
    for copy in copies:
        copy.wait()
    total = jnp.sum(marks[...].astype(F32), axis=0)
    inv0 = total[0:1] + total[1:2] + total[2:3]
    inv3 = total[3:4] + total[4:5] + total[5:6]
    ratio = total[6:7] + total[7:8]
    r = iota((DROWS, PORTS), 0)
    diag_ref[...] = jnp.where(r == 0, inv0, jnp.where(r == 1, inv3, 0.0))
    tile = 256
    for t in range(0, PORTS, tile):
        acc = jnp.dot(held[1], held[0, :, t : t + tile], preferred_element_type=F32)
        on = iota((PORTS, tile), 0) == iota((PORTS, tile), 1) + t
        mid = (jnp.where(on, ratio[:, t : t + tile], 0.0) - acc).astype(BF16)
        f_ref[:, t : t + tile] = jnp.dot(held[2], mid, preferred_element_type=F32).astype(BF16)


def fold(parts):
    return pl.pallas_call(
        fold_kernel,
        in_specs=[pl.BlockSpec(memory_space=pl.ANY)] * 8,
        out_shape=[pltpu.HBM((PORTS, PORTS), BF16), jax.ShapeDtypeStruct((DROWS, PORTS), F32)],
        scratch_shapes=[
            pltpu.VMEM((3, PORTS, PORTS), BF16),
            pltpu.VMEM((32, DROWS, PORTS), BF16),
            pltpu.SemaphoreType.DMA((4,)),
        ],
        compiler_params=params(32),
        cost_estimate=cost(4 * PORTS**3, 9 << 20),
        name="fold",
    )(*parts)


def finish_kernel(target_ref, ret_ref, f_ref, diag_ref, out_ref, route, response, scaled):
    step = pl.program_id(0)
    tile = ret_ref.shape[1]
    steps = PORTS // tile

    @pl.when(step == 0)
    def _():
        target = jnp.transpose(jnp.broadcast_to(target_ref[...], (128, ROWS)))
        for j in range(0, SLOTS, 128):
            route[:, j : j + 128] = jnp.where(iota((ROWS, 128), 1) + j == target, 1.0, 0.0).astype(BF16)

    @pl.when(step < steps)
    def _():
        at = pl.ds(pl.multiple_of(step * tile, tile), tile)
        piece = jnp.dot(route[...], ret_ref[...], preferred_element_type=F32)
        response[:, at] = piece
        scaled[:, at] = (piece * diag_ref[0:1, at]).astype(BF16)

    @pl.when(step >= steps)
    def _():
        at = pl.ds(pl.multiple_of((step - steps) * tile, tile), tile)
        coupled = lax.dot_general(scaled[...], f_ref[...], (((1,), (1,)), ((), ())), preferred_element_type=F32)
        out_ref[...] = response[:, at] * diag_ref[1:2, at] - coupled


def finish(target, returned, f, diag):
    tile = 256
    steps = PORTS // tile
    late = lambda i: jnp.maximum(i - steps, 0)
    return pl.pallas_call(
        finish_kernel,
        grid=(2 * steps,),
        in_specs=[
            whole(1, ROWS),
            pl.BlockSpec((SLOTS, tile), lambda i: (0, jnp.minimum(i, steps - 1))),
            pl.BlockSpec((tile, PORTS), lambda i: (late(i), 0)),
            whole(DROWS, PORTS),
        ],
        out_specs=pl.BlockSpec((ROWS, tile), lambda i: (0, late(i))),
        out_shape=pltpu.HBM((ROWS, PORTS), F32),
        scratch_shapes=[
            pltpu.VMEM((ROWS, SLOTS), BF16),
            pltpu.VMEM((ROWS, PORTS), F32),
            pltpu.VMEM((ROWS, PORTS), BF16),
        ],
        compiler_params=params(),
        cost_estimate=cost(4 * ROWS * PORTS * PORTS, 6 << 20),
        name="finish",
    )(target, returned, hbm(f), diag)


def group_swap(value, mask):
    return lax.ppermute(value, "group", [(i, i ^ mask) for i in range(8)])


def chip_shift(value, step, turn):
    pairs = []
    for o in range(OWNERS):
        c, x, y = o & 1, (o >> 1) & 3, o >> 3
        if (c ^ turn) == 0:
            x = (x + step) % 4
        else:
            y = (y + step) % 4
        pairs.append((o, (y * 4 + x) * 2 + c))
    return lax.ppermute(value, "owner", pairs)


def core_swap(value):
    return lax.ppermute(value, "owner", [(o, o ^ 1) for o in range(OWNERS)])


def exchange(value):
    shape = value.shape
    value = value.reshape(OWNERS, CAP, PORTS)
    return lax.all_to_all(value, "owner", split_axis=0, concat_axis=0, tiled=True).reshape(shape)


def body(port_rows, defect_owner, defect_half, defect_port, subcircuit_maps, schur_off, schur_diag, pivot_order):
    z0 = label(schur_off, schur_diag.reshape(1, OWN))
    z1, z2, z3 = (group_swap(z0, mask) for mask in (1, 2, 3))
    outgoing, target = prep(
        defect_owner.reshape(1, ROWS), defect_half.reshape(1, ROWS), defect_port.reshape(1, ROWS), port_rows, z0
    )
    arrived = exchange(outgoing)
    z, off, diag, gb = low_levels(z0, z1, z2, z3, pivot_order)
    pack = top_level(group_swap(z, 4), off, diag, gb, pivot_order)
    line = jnp.stack([pack] + [chip_shift(pack, step, 0) for step in STEPS])
    parts = [line] + [chip_shift(line, step, 1) for step in STEPS]
    parts = parts + [core_swap(part) for part in parts]
    f, inverses = fold(parts)
    answers = apply_maps(arrived, subcircuit_maps)
    returned = exchange(answers)
    return finish(target, returned, f, inverses)


def solution(mesh):
    return jax.shard_map(
        body,
        mesh=mesh,
        in_specs=(
            P(("group", "owner"), None),
            P(("group", "owner"), None),
            P(("group", "owner")),
            P(("group", "owner")),
            P(("group", "owner"), None, None),
            P(("group", "owner"), None),
            P(("group", "owner")),
            P(),
        ),
        out_specs=P(("group", "owner"), None),
        check_vma=False,
    )
```

```python
import jax
import jax.numpy as jnp
from jax import lax
from jax.experimental import pallas as pl
from jax.experimental.pallas import tpu as pltpu
from jax.sharding import PartitionSpec as P

BF16 = jnp.bfloat16
F32 = jnp.float32
I32 = jnp.int32

ROWS = 512
PORTS = 1024
OWNERS = 32
CAP = 32
SLOTS = OWNERS * CAP
OWN = 32
DROWS = 8
ZROWS = OWN + DROWS
PACK = 3 * OWN + DROWS
HALF_SCALE = 64.0
HALF_MARK = 32.0
STEPS = (1, -1, 2)
NEAR = (0, -1, 1, -2)
LINES = ((0, 0), (-1, 0), (1, 0), (2, 0), (2, 2))


def iota(shape, dim):
    return lax.broadcasted_iota(I32, shape, dim)


def params(limit=20, dims=None):
    return pltpu.CompilerParams(vmem_limit_bytes=limit << 20, dimension_semantics=dims)


def cost(flops, nbytes):
    return pl.CostEstimate(flops=flops, bytes_accessed=nbytes, transcendentals=0)


def hbm(value):
    return pltpu.with_memory_space_constraint(value, pltpu.HBM)


def vmem(value):
    return pltpu.with_memory_space_constraint(value, pltpu.VMEM)


ANYWHERE = pl.BlockSpec(memory_space=pl.ANY)
IN_VMEM = pl.BlockSpec(memory_space=pltpu.VMEM)


def split(value, parts):
    pieces = []
    for _ in range(parts):
        piece = value.astype(BF16).astype(F32)
        pieces.append(piece)
        value = value - piece
    return pieces


def rows_of(pieces, count):
    r = iota((count, PORTS), 0)
    out = jnp.zeros((count, PORTS), F32)
    for k, piece in enumerate(pieces):
        out = jnp.where(r == k, piece, out)
    return out.astype(BF16)


def own_lanes():
    own = lax.axis_index("owner")
    return iota((OWN, PORTS), 1) == own * OWN + iota((OWN, PORTS), 0)


def label_kernel(off_ref, diag_ref, z_ref):
    z_ref[:OWN, :] = off_ref[...]
    diag = jnp.sum(jnp.where(iota((OWN, OWN), 0) == iota((OWN, OWN), 1), diag_ref[...], 0.0), axis=1, keepdims=True)
    placed = jnp.sum(jnp.where(own_lanes(), diag, 0.0), axis=0, keepdims=True)
    z_ref[OWN:, :] = rows_of(split(placed, 3), DROWS)


def label(off, diag):
    return pl.pallas_call(
        label_kernel,
        out_shape=jax.ShapeDtypeStruct((ZROWS, PORTS), BF16),
        compiler_params=params(),
        cost_estimate=cost(OWN * PORTS, 1 << 17),
        name="label",
    )(hbm(off), hbm(diag))


def prep_kernel(
    owner_ref, half_ref, port_ref, rows_ref, out_ref, target_ref, names, rows, stim, made, in_sems, out_sems
):
    small = [
        pltpu.make_async_copy(ref, names.at[k], in_sems.at[2 + k]) for k, ref in enumerate((owner_ref, half_ref, port_ref))
    ]
    for copy in small:
        copy.start()
    half_rows = ROWS // 2
    loads = [
        pltpu.make_async_copy(rows_ref.at[r : r + half_rows], rows.at[r : r + half_rows], in_sems.at[k])
        for k, r in enumerate(range(0, ROWS, half_rows))
    ]
    for load in loads:
        load.start()
    for copy in small:
        copy.wait()
    owner = names[0]
    named = iota((OWNERS, ROWS), 0) == owner
    earlier = jnp.where(iota((ROWS, ROWS), 0) < iota((ROWS, ROWS), 1), 1.0, 0.0).astype(BF16)
    before = jnp.dot(jnp.where(named, 1.0, 0.0).astype(BF16), earlier, preferred_element_type=F32)
    rank = jnp.sum(jnp.where(named, before, 0.0), axis=0, keepdims=True)
    target = owner * CAP + rank.astype(I32)
    target_ref[...] = target + SLOTS * names[1]
    scale = jnp.where(names[1] == 1, HALF_SCALE, 1.0)
    port = jnp.transpose(jnp.broadcast_to(names[2], (128, ROWS)))
    for k, load in enumerate(loads):
        load.wait()
        at = slice(k * half_rows, (k + 1) * half_rows)
        for j in range(0, PORTS, 128):
            lanes = slice(j, j + 128)
            bump = jnp.where(iota((half_rows, 128), 1) + j == port[at], 8.0, 0.0)
            stim[at, lanes] = (rows[at, lanes].astype(F32) + bump).astype(BF16)
    stores = []
    tile = 256
    for k, u in enumerate(range(0, SLOTS, tile)):
        route = jnp.where(iota((tile, ROWS), 0) + u == target, scale, 0.0).astype(BF16)
        made[u : u + tile, :] = jnp.dot(route, stim[...], preferred_element_type=F32).astype(BF16)
        store = pltpu.make_async_copy(made.at[u : u + tile], out_ref.at[u : u + tile], out_sems.at[k])
        store.start()
        stores.append(store)
    for store in stores:
        store.wait()


def prep(owner, half, port, rows):
    return pl.pallas_call(
        prep_kernel,
        in_specs=[ANYWHERE] * 4,
        out_specs=[ANYWHERE, IN_VMEM],
        out_shape=[pltpu.HBM((SLOTS, PORTS), BF16), jax.ShapeDtypeStruct((1, ROWS), I32)],
        scratch_shapes=[
            pltpu.VMEM((3, 1, ROWS), I32),
            pltpu.VMEM((ROWS, PORTS), BF16),
            pltpu.VMEM((ROWS, PORTS), BF16),
            pltpu.VMEM((SLOTS, PORTS), BF16),
            pltpu.SemaphoreType.DMA((5,)),
            pltpu.SemaphoreType.DMA((4,)),
        ],
        compiler_params=params(),
        cost_estimate=cost(2 * SLOTS * ROWS * PORTS, 4 << 20),
        name="prep",
    )(hbm(owner), hbm(half), hbm(port), hbm(rows))


def maps_kernel(x_ref, maps_ref, out_ref, maps, first, other, total, made, in_sems, out_sems):
    tile = 256
    tiles = SLOTS // tile
    loads = [
        pltpu.make_async_copy(maps_ref.at[h, r : r + tile], maps.at[h, r : r + tile], in_sems.at[h, k])
        for h in range(2)
        for k, r in enumerate(range(0, PORTS, tile))
    ]
    for load in loads[:tiles]:
        load.start()
    for r in range(0, SLOTS, tile):
        x = x_ref[r : r + tile, :]
        peak = jnp.abs(x[:, :128])
        for j in range(128, PORTS, 128):
            peak = jnp.maximum(peak, jnp.abs(x[:, j : j + 128]))
        second = jnp.max(peak.astype(F32), axis=1, keepdims=True) > HALF_MARK
        keep = jnp.where(second, 0.0, 1.0).astype(BF16)
        kept = x * keep
        first[r : r + tile, :] = kept
        other[r : r + tile, :] = x - kept
    for load in loads[tiles:]:
        load.start()
    for load in loads[:tiles]:
        load.wait()
    for n in range(0, PORTS, tile):
        total[:, n : n + tile] = jnp.dot(first[...], maps[0, :, n : n + tile], preferred_element_type=F32)
    for load in loads[tiles:]:
        load.wait()
    stores = []
    for k, r in enumerate(range(0, SLOTS, tile)):
        at = slice(r, r + tile)
        made[at, :] = (total[at, :] + jnp.dot(other[at, :], maps[1], preferred_element_type=F32)).astype(BF16)
        store = pltpu.make_async_copy(made.at[at], out_ref.at[at], out_sems.at[k])
        store.start()
        stores.append(store)
    for store in stores:
        store.wait()


def apply_maps(x, maps):
    return pl.pallas_call(
        maps_kernel,
        in_specs=[IN_VMEM, ANYWHERE],
        out_specs=ANYWHERE,
        out_shape=pltpu.HBM((SLOTS, PORTS), BF16),
        scratch_shapes=[
            pltpu.VMEM((2, PORTS, PORTS), BF16),
            pltpu.VMEM((SLOTS, PORTS), BF16),
            pltpu.VMEM((SLOTS, PORTS), BF16),
            pltpu.VMEM((SLOTS, PORTS), F32),
            pltpu.VMEM((SLOTS, PORTS), BF16),
            pltpu.SemaphoreType.DMA((2, 4)),
            pltpu.SemaphoreType.DMA((4,)),
        ],
        compiler_params=params(28),
        cost_estimate=cost(4 * SLOTS * PORTS * PORTS, 8 << 20),
        name="apply_maps",
    )(vmem(x), hbm(maps))


def permuted(values, order):
    out = jnp.zeros(values.shape, F32)
    for j in range(0, PORTS, 256):
        pick = jnp.where(iota((256, PORTS), 0) + j == order, 1.0, 0.0).astype(BF16)
        out = out + jnp.dot(values[:, j : j + 256], pick, preferred_element_type=F32)
    return out


def read_diag(z_ref):
    z = z_ref[OWN:, :].astype(F32)
    return z[0:1] + z[1:2] + z[2:3]


def column(placed):
    return jnp.sum(jnp.where(own_lanes(), placed, 0.0), axis=1, keepdims=True)


def inverse(placed):
    held = placed > 0.0
    return jnp.where(held, 1.0 / jnp.where(held, placed, 1.0), 0.0)


def low_levels_kernel(z0_ref, z1_ref, z2_ref, z3_ref, order_ref, z_ref, off_ref, diag_ref, gb_ref):
    picked = permuted(jnp.concatenate([z1_ref[:OWN, :], z3_ref[:OWN, :]], axis=0), order_ref[0:1, :])
    off1 = z0_ref[:OWN, :].astype(F32) + picked[:OWN]
    picked2 = permuted(jnp.concatenate([z2_ref[:OWN, :], picked[OWN:].astype(BF16)], axis=0), order_ref[1:2, :])
    off2 = off1 + (picked2[:OWN] + picked2[OWN:])
    d0 = read_diag(z0_ref)
    d1 = d0 + read_diag(z1_ref)
    d2 = d1 + (read_diag(z2_ref) + read_diag(z3_ref))
    z_ref[:OWN, :] = off2.astype(BF16)
    z_ref[OWN:, :] = rows_of(split(d2, 3), DROWS)
    off_ref[...] = off2
    r = iota((DROWS, PORTS), 0)
    diag_ref[...] = jnp.where(r == 0, d0, jnp.where(r == 1, d2, 0.0))
    gb_ref[:OWN, :] = ((jnp.where(own_lanes(), d0, 0.0) - off1) / column(d1)).astype(BF16)
    gb_ref[OWN:, :] = (off2 / column(d2)).astype(BF16)


def low_levels(z0, z1, z2, z3, order):
    return pl.pallas_call(
        low_levels_kernel,
        out_shape=[
            jax.ShapeDtypeStruct((ZROWS, PORTS), BF16),
            jax.ShapeDtypeStruct((OWN, PORTS), F32),
            jax.ShapeDtypeStruct((DROWS, PORTS), F32),
            jax.ShapeDtypeStruct((2 * OWN, PORTS), BF16),
        ],
        compiler_params=params(),
        cost_estimate=cost(4 * 64 * PORTS * PORTS, 1 << 20),
        name="low_levels",
    )(z0, z1, z2, z3, order)


def top_level_kernel(z4_ref, off_ref, diag_ref, gb_ref, order_ref, pack_ref):
    off3 = off_ref[...] + permuted(z4_ref[:OWN, :], order_ref[2:3, :])
    d0, d2 = diag_ref[0:1, :], diag_ref[1:2, :]
    d3 = d2 + read_diag(z4_ref)
    pack_ref[: 2 * OWN, :] = gb_ref[...]
    pack_ref[2 * OWN : 3 * OWN, :] = (off3 / column(d3)).astype(BF16)
    pieces = split(inverse(d0), 3) + split(inverse(d3), 3) + split(d0 * inverse(d2), 2)
    pack_ref[3 * OWN :, :] = rows_of(pieces, DROWS)


def top_level(z4, off, diag, gb, order):
    return pl.pallas_call(
        top_level_kernel,
        out_shape=jax.ShapeDtypeStruct((PACK, PORTS), BF16),
        compiler_params=params(),
        cost_estimate=cost(2 * 32 * PORTS * PORTS, 1 << 20),
        name="top_level",
    )(z4, off, diag, gb, order)


def fold_kernel(*refs):
    parts, (f_ref, diag_ref, held, marks) = refs[: 2 * len(LINES)], refs[2 * len(LINES) :]
    own = lax.axis_index("owner")
    core, x, y = own & 1, (own >> 1) & 3, own >> 3
    slot = 0
    for side in range(2):
        c = core if side == 0 else 1 - core
        for m, (away, first) in enumerate(LINES):
            for k in range(parts[side * len(LINES) + m].shape[0]):
                dx = jnp.where(c == 0, NEAR[k + first], away)
                dy = jnp.where(c == 0, away, NEAR[k + first])
                start = ((((y + dy) & 3) * 4 + ((x + dx) & 3)) * 2 + c) * OWN
                at = pl.ds(pl.multiple_of(start, OWN), OWN)
                block = parts[side * len(LINES) + m]
                for j in range(3):
                    held[j, at, :] = block[k, j * OWN : (j + 1) * OWN, :]
                marks[slot] = block[k, 3 * OWN :, :]
                slot += 1
    total = jnp.sum(marks[...].astype(F32), axis=0)
    inv0 = total[0:1] + total[1:2] + total[2:3]
    inv3 = total[3:4] + total[4:5] + total[5:6]
    ratio = total[6:7] + total[7:8]
    r = iota((DROWS, PORTS), 0)
    diag_ref[...] = jnp.where(r == 0, inv0, jnp.where(r == 1, inv3, 0.0))
    tile = 256
    for t in range(0, PORTS, tile):
        acc = jnp.dot(held[1], held[0, :, t : t + tile], preferred_element_type=F32)
        on = iota((PORTS, tile), 0) == iota((PORTS, tile), 1) + t
        mid = (jnp.where(on, ratio[:, t : t + tile], 0.0) - acc).astype(BF16)
        f_ref[t : t + tile, :] = jnp.transpose(jnp.dot(held[2], mid, preferred_element_type=F32)).astype(BF16)


def fold(parts):
    return pl.pallas_call(
        fold_kernel,
        in_specs=[IN_VMEM] * (2 * len(LINES)),
        out_shape=[pltpu.HBM((PORTS, PORTS), BF16), pltpu.VMEM((DROWS, PORTS), F32)],
        scratch_shapes=[
            pltpu.VMEM((3, PORTS, PORTS), BF16),
            pltpu.VMEM((32, DROWS, PORTS), BF16),
        ],
        compiler_params=params(24),
        cost_estimate=cost(4 * PORTS**3, 9 << 20),
        name="fold",
    )(*[vmem(part) for part in parts])


def finish_kernel(target_ref, ret_ref, f_ref, diag_ref, out_ref, route, response, scaled, coupling, made, in_sem, out_sems):
    load = pltpu.make_async_copy(f_ref, coupling, in_sem)
    load.start()
    code = jnp.transpose(jnp.broadcast_to(target_ref[...], (128, ROWS)))
    scale = jnp.where(code >= SLOTS, 1.0 / HALF_SCALE, 1.0)
    target = code & (SLOTS - 1)
    for j in range(0, SLOTS, 128):
        route[:, j : j + 128] = jnp.where(iota((ROWS, 128), 1) + j == target, scale, 0.0).astype(BF16)
    for n in range(0, PORTS, 256):
        at = slice(n, n + 256)
        piece = jnp.dot(route[...], ret_ref[:, at], preferred_element_type=F32)
        response[:, at] = piece
        scaled[:, at] = (piece * diag_ref[0:1, at]).astype(BF16)
    load.wait()
    stores = []
    tile = 128
    for k, r in enumerate(range(0, ROWS, tile)):
        at = slice(r, r + tile)
        coupled = jnp.dot(scaled[at, :], coupling[...], preferred_element_type=F32)
        made[at, :] = response[at, :] * diag_ref[1:2, :] - coupled
        store = pltpu.make_async_copy(made.at[at], out_ref.at[at], out_sems.at[k])
        store.start()
        stores.append(store)
    for store in stores:
        store.wait()


def finish(target, returned, f, diag):
    return pl.pallas_call(
        finish_kernel,
        in_specs=[IN_VMEM, IN_VMEM, ANYWHERE, IN_VMEM],
        out_specs=ANYWHERE,
        out_shape=pltpu.HBM((ROWS, PORTS), F32),
        scratch_shapes=[
            pltpu.VMEM((ROWS, SLOTS), BF16),
            pltpu.VMEM((ROWS, PORTS), F32),
            pltpu.VMEM((ROWS, PORTS), BF16),
            pltpu.VMEM((PORTS, PORTS), BF16),
            pltpu.VMEM((ROWS, PORTS), F32),
            pltpu.SemaphoreType.DMA,
            pltpu.SemaphoreType.DMA((4,)),
        ],
        compiler_params=params(24),
        cost_estimate=cost(4 * ROWS * PORTS * PORTS, 6 << 20),
        name="finish",
    )(vmem(target), vmem(returned), hbm(f), vmem(diag))


def group_swap(value, mask):
    return lax.ppermute(value, "group", [(i, i ^ mask) for i in range(8)])


def chip_shift(value, step, turn):
    pairs = []
    for o in range(OWNERS):
        c, x, y = o & 1, (o >> 1) & 3, o >> 3
        if (c ^ turn) == 0:
            x = (x + step) % 4
        else:
            y = (y + step) % 4
        pairs.append((o, (y * 4 + x) * 2 + c))
    return lax.ppermute(value, "owner", pairs)


def core_swap(value):
    return lax.ppermute(value, "owner", [(o, o ^ 1) for o in range(OWNERS)])


def exchange(value):
    shape = value.shape
    value = value.reshape(OWNERS, CAP, PORTS)
    return lax.all_to_all(value, "owner", split_axis=0, concat_axis=0, tiled=True).reshape(shape)


def body(port_rows, defect_owner, defect_half, defect_port, subcircuit_maps, schur_off, schur_diag, pivot_order):
    z0 = label(schur_off, schur_diag.reshape(1, OWN))
    z1, z2, z3 = (group_swap(z0, mask) for mask in (1, 2, 3))
    outgoing, target = prep(
        defect_owner.reshape(1, ROWS), defect_half.reshape(1, ROWS), defect_port.reshape(1, ROWS), port_rows
    )
    arrived = exchange(outgoing)
    z, off, diag, gb = low_levels(z0, z1, z2, z3, pivot_order)
    pack = top_level(group_swap(z, 4), off, diag, gb, pivot_order)
    line = jnp.stack([pack] + [chip_shift(pack, step, 0) for step in STEPS])
    left, right = chip_shift(line, 1, 1), chip_shift(line, -1, 1)
    far_low, far_high = chip_shift(left[:2], 1, 1), chip_shift(right[2:], -1, 1)
    parts = [line, left, right, far_low, far_high]
    parts = parts + [core_swap(part) for part in parts]
    f, inverses = fold(parts)
    answers = apply_maps(arrived, subcircuit_maps)
    returned = exchange(answers)
    return finish(target, returned, f, inverses)


def solution(mesh):
    return jax.shard_map(
        body,
        mesh=mesh,
        in_specs=(
            P(("group", "owner"), None),
            P(("group", "owner"), None),
            P(("group", "owner")),
            P(("group", "owner")),
            P(("group", "owner"), None, None),
            P(("group", "owner"), None),
            P(("group", "owner")),
            P(),
        ),
        out_specs=P(("group", "owner"), None),
        check_vma=False,
    )
```

```python
import jax
import jax.numpy as jnp
from jax import lax
from jax.experimental import pallas as pl
from jax.experimental.pallas import tpu as pltpu
from jax.sharding import PartitionSpec as P

BF16 = jnp.bfloat16
F32 = jnp.float32
I32 = jnp.int32

ROWS = 512
PORTS = 1024
OWNERS = 32
CAP = 32
SLOTS = OWNERS * CAP
OWN = 32
DROWS = 8
ZROWS = OWN + DROWS
PACK = 3 * OWN + DROWS
HALF_SCALE = 64.0
HALF_MARK = 32.0
STEPS = (1, -1, 2)
NEAR = (0, -1, 1, -2)
LINES = ((0, 0), (-1, 0), (1, 0), (2, 0), (2, 2))


def iota(shape, dim):
    return lax.broadcasted_iota(I32, shape, dim)


def params(limit=20, dims=None):
    return pltpu.CompilerParams(vmem_limit_bytes=limit << 20, dimension_semantics=dims)


def cost(flops, nbytes):
    return pl.CostEstimate(flops=flops, bytes_accessed=nbytes, transcendentals=0)


def hbm(value):
    return pltpu.with_memory_space_constraint(value, pltpu.HBM)


def vmem(value):
    return pltpu.with_memory_space_constraint(value, pltpu.VMEM)


ANYWHERE = pl.BlockSpec(memory_space=pl.ANY)
IN_VMEM = pl.BlockSpec(memory_space=pltpu.VMEM)


def split(value, parts):
    pieces = []
    for _ in range(parts):
        piece = value.astype(BF16).astype(F32)
        pieces.append(piece)
        value = value - piece
    return pieces


def rows_of(pieces, count):
    r = iota((count, PORTS), 0)
    out = jnp.zeros((count, PORTS), F32)
    for k, piece in enumerate(pieces):
        out = jnp.where(r == k, piece, out)
    return out.astype(BF16)


def own_lanes():
    own = lax.axis_index("owner")
    return iota((OWN, PORTS), 1) == own * OWN + iota((OWN, PORTS), 0)


def label_kernel(off_ref, diag_ref, z_ref):
    z_ref[:OWN, :] = off_ref[...]
    diag = jnp.sum(jnp.where(iota((OWN, OWN), 0) == iota((OWN, OWN), 1), diag_ref[...], 0.0), axis=1, keepdims=True)
    placed = jnp.sum(jnp.where(own_lanes(), diag, 0.0), axis=0, keepdims=True)
    z_ref[OWN:, :] = rows_of(split(placed, 3), DROWS)


def label(off, diag):
    return pl.pallas_call(
        label_kernel,
        out_shape=jax.ShapeDtypeStruct((ZROWS, PORTS), BF16),
        compiler_params=params(),
        cost_estimate=cost(OWN * PORTS, 1 << 17),
        name="label",
    )(hbm(off), hbm(diag))


def prep_kernel(
    owner_ref, half_ref, port_ref, rows_ref, out_ref, target_ref, names, rows, stim, made, in_sems, out_sems
):
    small = [
        pltpu.make_async_copy(ref, names.at[k], in_sems.at[2 + k]) for k, ref in enumerate((owner_ref, half_ref, port_ref))
    ]
    for copy in small:
        copy.start()
    half_rows = ROWS // 2
    loads = [
        pltpu.make_async_copy(rows_ref.at[r : r + half_rows], rows.at[r : r + half_rows], in_sems.at[k])
        for k, r in enumerate(range(0, ROWS, half_rows))
    ]
    for load in loads:
        load.start()
    for copy in small:
        copy.wait()
    owner = names[0]
    named = iota((OWNERS, ROWS), 0) == owner
    earlier = jnp.where(iota((ROWS, ROWS), 0) < iota((ROWS, ROWS), 1), 1.0, 0.0).astype(BF16)
    before = jnp.dot(jnp.where(named, 1.0, 0.0).astype(BF16), earlier, preferred_element_type=F32)
    rank = jnp.sum(jnp.where(named, before, 0.0), axis=0, keepdims=True)
    target = owner * CAP + rank.astype(I32)
    target_ref[...] = target + SLOTS * names[1]
    scale = jnp.where(names[1] == 1, HALF_SCALE, 1.0)
    port = jnp.transpose(jnp.broadcast_to(names[2], (128, ROWS)))
    for k, load in enumerate(loads):
        load.wait()
        at = slice(k * half_rows, (k + 1) * half_rows)
        for j in range(0, PORTS, 128):
            lanes = slice(j, j + 128)
            bump = jnp.where(iota((half_rows, 128), 1) + j == port[at], 8.0, 0.0)
            stim[at, lanes] = (rows[at, lanes].astype(F32) + bump).astype(BF16)
    stores = []
    tile = 256
    for k, u in enumerate(range(0, SLOTS, tile)):
        route = jnp.where(iota((tile, ROWS), 0) + u == target, scale, 0.0).astype(BF16)
        made[u : u + tile, :] = jnp.dot(route, stim[...], preferred_element_type=F32).astype(BF16)
        store = pltpu.make_async_copy(made.at[u : u + tile], out_ref.at[u : u + tile], out_sems.at[k])
        store.start()
        stores.append(store)
    for store in stores:
        store.wait()


def prep(owner, half, port, rows):
    return pl.pallas_call(
        prep_kernel,
        in_specs=[ANYWHERE] * 4,
        out_specs=[ANYWHERE, IN_VMEM],
        out_shape=[pltpu.HBM((SLOTS, PORTS), BF16), jax.ShapeDtypeStruct((1, ROWS), I32)],
        scratch_shapes=[
            pltpu.VMEM((3, 1, ROWS), I32),
            pltpu.VMEM((ROWS, PORTS), BF16),
            pltpu.VMEM((ROWS, PORTS), BF16),
            pltpu.VMEM((SLOTS, PORTS), BF16),
            pltpu.SemaphoreType.DMA((5,)),
            pltpu.SemaphoreType.DMA((4,)),
        ],
        compiler_params=params(),
        cost_estimate=cost(2 * SLOTS * ROWS * PORTS, 4 << 20),
        name="prep",
    )(hbm(owner), hbm(half), hbm(port), hbm(rows))


def maps_kernel(x_ref, maps_ref, out_ref, maps, first, other, total, made, in_sems, out_sems):
    tile = 256
    tiles = SLOTS // tile
    loads = [
        pltpu.make_async_copy(maps_ref.at[h, r : r + tile], maps.at[h, r : r + tile], in_sems.at[h, k])
        for h in range(2)
        for k, r in enumerate(range(0, PORTS, tile))
    ]
    for load in loads[:tiles]:
        load.start()
    for r in range(0, SLOTS, tile):
        x = x_ref[r : r + tile, :]
        peak = jnp.abs(x[:, :128])
        for j in range(128, PORTS, 128):
            peak = jnp.maximum(peak, jnp.abs(x[:, j : j + 128]))
        second = jnp.max(peak.astype(F32), axis=1, keepdims=True) > HALF_MARK
        keep = jnp.where(second, 0.0, 1.0).astype(BF16)
        kept = x * keep
        first[r : r + tile, :] = kept
        other[r : r + tile, :] = x - kept
    for load in loads[tiles:]:
        load.start()
    for load in loads[:tiles]:
        load.wait()
    for n in range(0, PORTS, tile):
        total[:, n : n + tile] = jnp.dot(first[...], maps[0, :, n : n + tile], preferred_element_type=F32)
    for load in loads[tiles:]:
        load.wait()
    stores = []
    for k, r in enumerate(range(0, SLOTS, tile)):
        at = slice(r, r + tile)
        made[at, :] = (total[at, :] + jnp.dot(other[at, :], maps[1], preferred_element_type=F32)).astype(BF16)
        store = pltpu.make_async_copy(made.at[at], out_ref.at[at], out_sems.at[k])
        store.start()
        stores.append(store)
    for store in stores:
        store.wait()


def apply_maps(x, maps):
    return pl.pallas_call(
        maps_kernel,
        in_specs=[IN_VMEM, ANYWHERE],
        out_specs=ANYWHERE,
        out_shape=pltpu.HBM((SLOTS, PORTS), BF16),
        scratch_shapes=[
            pltpu.VMEM((2, PORTS, PORTS), BF16),
            pltpu.VMEM((SLOTS, PORTS), BF16),
            pltpu.VMEM((SLOTS, PORTS), BF16),
            pltpu.VMEM((SLOTS, PORTS), F32),
            pltpu.VMEM((SLOTS, PORTS), BF16),
            pltpu.SemaphoreType.DMA((2, 4)),
            pltpu.SemaphoreType.DMA((4,)),
        ],
        compiler_params=params(28),
        cost_estimate=cost(4 * SLOTS * PORTS * PORTS, 8 << 20),
        name="apply_maps",
    )(vmem(x), hbm(maps))


def permuted(values, order):
    out = jnp.zeros(values.shape, F32)
    for j in range(0, PORTS, 256):
        pick = jnp.where(iota((256, PORTS), 0) + j == order, 1.0, 0.0).astype(BF16)
        out = out + jnp.dot(values[:, j : j + 256], pick, preferred_element_type=F32)
    return out


def read_diag(z_ref):
    z = z_ref[OWN:, :].astype(F32)
    return z[0:1] + z[1:2] + z[2:3]


def column(placed):
    return jnp.sum(jnp.where(own_lanes(), placed, 0.0), axis=1, keepdims=True)


def inverse(placed):
    held = placed > 0.0
    return jnp.where(held, 1.0 / jnp.where(held, placed, 1.0), 0.0)


def low_levels_kernel(z0_ref, z1_ref, z2_ref, z3_ref, order_ref, z_ref, off_ref, diag_ref, gb_ref):
    picked = permuted(jnp.concatenate([z1_ref[:OWN, :], z3_ref[:OWN, :]], axis=0), order_ref[0:1, :])
    off1 = z0_ref[:OWN, :].astype(F32) + picked[:OWN]
    picked2 = permuted(jnp.concatenate([z2_ref[:OWN, :], picked[OWN:].astype(BF16)], axis=0), order_ref[1:2, :])
    off2 = off1 + (picked2[:OWN] + picked2[OWN:])
    d0 = read_diag(z0_ref)
    d1 = d0 + read_diag(z1_ref)
    d2 = d1 + (read_diag(z2_ref) + read_diag(z3_ref))
    z_ref[:OWN, :] = off2.astype(BF16)
    z_ref[OWN:, :] = rows_of(split(d2, 3), DROWS)
    off_ref[...] = off2
    r = iota((DROWS, PORTS), 0)
    diag_ref[...] = jnp.where(r == 0, d0, jnp.where(r == 1, d2, 0.0))
    gb_ref[:OWN, :] = ((jnp.where(own_lanes(), d0, 0.0) - off1) / column(d1)).astype(BF16)
    gb_ref[OWN:, :] = (off2 / column(d2)).astype(BF16)


def low_levels(z0, z1, z2, z3, order):
    return pl.pallas_call(
        low_levels_kernel,
        out_shape=[
            jax.ShapeDtypeStruct((ZROWS, PORTS), BF16),
            jax.ShapeDtypeStruct((OWN, PORTS), F32),
            jax.ShapeDtypeStruct((DROWS, PORTS), F32),
            jax.ShapeDtypeStruct((2 * OWN, PORTS), BF16),
        ],
        compiler_params=params(),
        cost_estimate=cost(4 * 64 * PORTS * PORTS, 1 << 20),
        name="low_levels",
    )(z0, z1, z2, z3, order)


def top_level_kernel(z4_ref, off_ref, diag_ref, gb_ref, order_ref, pack_ref):
    off3 = off_ref[...] + permuted(z4_ref[:OWN, :], order_ref[2:3, :])
    d0, d2 = diag_ref[0:1, :], diag_ref[1:2, :]
    d3 = d2 + read_diag(z4_ref)
    pack_ref[: 2 * OWN, :] = gb_ref[...]
    pack_ref[2 * OWN : 3 * OWN, :] = (off3 / column(d3)).astype(BF16)
    pieces = split(inverse(d0), 3) + split(inverse(d3), 3) + split(d0 * inverse(d2), 2)
    pack_ref[3 * OWN :, :] = rows_of(pieces, DROWS)


def top_level(z4, off, diag, gb, order):
    return pl.pallas_call(
        top_level_kernel,
        out_shape=jax.ShapeDtypeStruct((PACK, PORTS), BF16),
        compiler_params=params(),
        cost_estimate=cost(2 * 32 * PORTS * PORTS, 1 << 20),
        name="top_level",
    )(z4, off, diag, gb, order)


def finish_kernel(target_ref, ret_ref, *refs):
    pieces = 2 * len(LINES)
    parts = refs[:pieces]
    out_ref, route, held, marks, response, panel, made, out_sems = refs[pieces:]
    code = jnp.transpose(jnp.broadcast_to(target_ref[...], (128, ROWS)))
    scale = jnp.where(code >= SLOTS, 1.0 / HALF_SCALE, 1.0)
    target = code & (SLOTS - 1)
    for j in range(0, SLOTS, 128):
        route[:, j : j + 128] = jnp.where(iota((ROWS, 128), 1) + j == target, scale, 0.0).astype(BF16)
    own = lax.axis_index("owner")
    core, x, y = own & 1, (own >> 1) & 3, own >> 3
    slot = 0
    for side in range(2):
        c = core if side == 0 else 1 - core
        for m, (away, first) in enumerate(LINES):
            block = parts[side * len(LINES) + m]
            for k in range(block.shape[0]):
                dx = jnp.where(c == 0, NEAR[k + first], away)
                dy = jnp.where(c == 0, away, NEAR[k + first])
                start = ((((y + dy) & 3) * 4 + ((x + dx) & 3)) * 2 + c) * OWN
                at = pl.ds(pl.multiple_of(start, OWN), OWN)
                for j in range(3):
                    held[j, at, :] = block[k, j * OWN : (j + 1) * OWN, :]
                marks[slot] = block[k, 3 * OWN :, :]
                slot += 1
    total = jnp.sum(marks[...].astype(F32), axis=0)
    inv0 = total[0:1] + total[1:2] + total[2:3]
    inv3 = total[3:4] + total[4:5] + total[5:6]
    inv2 = inv0 * (total[6:7] + total[7:8])
    wide = 256
    for n in range(0, PORTS, wide):
        at = slice(n, n + wide)
        piece = jnp.dot(route[...], ret_ref[:, at], preferred_element_type=F32)
        response[:, at] = piece
        panel[0, :, at] = (piece * inv0[:, at]).astype(BF16)
    for n in range(0, PORTS, wide):
        at = slice(n, n + wide)
        panel[1, :, at] = across(panel[0], held[0, at, :]).astype(BF16)
    for n in range(0, PORTS, wide):
        at = slice(n, n + wide)
        panel[0, :, at] = (response[:, at] * inv2[:, at] - across(panel[1], held[1, at, :])).astype(BF16)
    stores = []
    tile = 256
    for k, r in enumerate(range(0, ROWS, tile)):
        at = slice(r, r + tile)
        made[at, :] = response[at, :] * inv3 - across(panel[0, at, :], held[2])
        store = pltpu.make_async_copy(made.at[at], out_ref.at[at], out_sems.at[k])
        store.start()
        stores.append(store)
    for store in stores:
        store.wait()


def across(rows, matrix):
    return lax.dot_general(rows, matrix, (((1,), (1,)), ((), ())), preferred_element_type=F32)


def finish(target, returned, parts):
    return pl.pallas_call(
        finish_kernel,
        in_specs=[IN_VMEM] * (2 + len(parts)),
        out_specs=ANYWHERE,
        out_shape=pltpu.HBM((ROWS, PORTS), F32),
        scratch_shapes=[
            pltpu.VMEM((ROWS, SLOTS), BF16),
            pltpu.VMEM((3, PORTS, PORTS), BF16),
            pltpu.VMEM((32, DROWS, PORTS), BF16),
            pltpu.VMEM((ROWS, PORTS), F32),
            pltpu.VMEM((2, ROWS, PORTS), BF16),
            pltpu.VMEM((ROWS, PORTS), F32),
            pltpu.SemaphoreType.DMA((2,)),
        ],
        compiler_params=params(28),
        cost_estimate=cost(8 * ROWS * PORTS * PORTS, 6 << 20),
        name="finish",
    )(vmem(target), vmem(returned), *[vmem(part) for part in parts])


def group_swap(value, mask):
    return lax.ppermute(value, "group", [(i, i ^ mask) for i in range(8)])


def chip_shift(value, step, turn):
    pairs = []
    for o in range(OWNERS):
        c, x, y = o & 1, (o >> 1) & 3, o >> 3
        if (c ^ turn) == 0:
            x = (x + step) % 4
        else:
            y = (y + step) % 4
        pairs.append((o, (y * 4 + x) * 2 + c))
    return lax.ppermute(value, "owner", pairs)


def core_swap(value):
    return lax.ppermute(value, "owner", [(o, o ^ 1) for o in range(OWNERS)])


def exchange(value):
    shape = value.shape
    value = value.reshape(OWNERS, CAP, PORTS)
    return lax.all_to_all(value, "owner", split_axis=0, concat_axis=0, tiled=True).reshape(shape)


def body(port_rows, defect_owner, defect_half, defect_port, subcircuit_maps, schur_off, schur_diag, pivot_order):
    z0 = label(schur_off, schur_diag.reshape(1, OWN))
    z1, z2, z3 = (group_swap(z0, mask) for mask in (1, 2, 3))
    outgoing, target = prep(
        defect_owner.reshape(1, ROWS), defect_half.reshape(1, ROWS), defect_port.reshape(1, ROWS), port_rows
    )
    arrived = exchange(outgoing)
    z, off, diag, gb = low_levels(z0, z1, z2, z3, pivot_order)
    pack = top_level(group_swap(z, 4), off, diag, gb, pivot_order)
    line = jnp.stack([pack] + [chip_shift(pack, step, 0) for step in STEPS])
    left, right = chip_shift(line, 1, 1), chip_shift(line, -1, 1)
    far_low, far_high = chip_shift(left[:2], 1, 1), chip_shift(right[2:], -1, 1)
    parts = [line, left, right, far_low, far_high]
    parts = parts + [core_swap(part) for part in parts]
    answers = apply_maps(arrived, subcircuit_maps)
    returned = exchange(answers)
    return finish(target, returned, parts)


def solution(mesh):
    return jax.shard_map(
        body,
        mesh=mesh,
        in_specs=(
            P(("group", "owner"), None),
            P(("group", "owner"), None),
            P(("group", "owner")),
            P(("group", "owner")),
            P(("group", "owner"), None, None),
            P(("group", "owner"), None),
            P(("group", "owner")),
            P(),
        ),
        out_specs=P(("group", "owner"), None),
        check_vma=False,
    )
```

```python
import jax
import jax.numpy as jnp
from jax import lax
from jax.experimental import pallas as pl
from jax.experimental.pallas import tpu as pltpu
from jax.sharding import PartitionSpec as P

BF16 = jnp.bfloat16
F32 = jnp.float32
I32 = jnp.int32

ROWS = 512
PORTS = 1024
OWNERS = 32
CAP = 32
SLOTS = OWNERS * CAP
OWN = 32
DROWS = 8
ZROWS = OWN + DROWS
PACK = 3 * OWN + DROWS
HALF_SCALE = 64.0
HALF_MARK = 32.0
STEPS = (1, -1, 2)
NEAR = (0, -1, 1, -2)
NEAR_LINES = ((0, range(4)), (-1, range(4)), (1, range(4)))
FAR_LINES = ((2, range(2)), (2, range(2, 4)))


def iota(shape, dim):
    return lax.broadcasted_iota(I32, shape, dim)


def params(limit=20, dims=None):
    return pltpu.CompilerParams(vmem_limit_bytes=limit << 20, dimension_semantics=dims)


def cost(flops, nbytes):
    return pl.CostEstimate(flops=flops, bytes_accessed=nbytes, transcendentals=0)


def hbm(value):
    return pltpu.with_memory_space_constraint(value, pltpu.HBM)


def vmem(value):
    return pltpu.with_memory_space_constraint(value, pltpu.VMEM)


ANYWHERE = pl.BlockSpec(memory_space=pl.ANY)
IN_VMEM = pl.BlockSpec(memory_space=pltpu.VMEM)


def split(value, parts):
    pieces = []
    for _ in range(parts):
        piece = value.astype(BF16).astype(F32)
        pieces.append(piece)
        value = value - piece
    return pieces


def rows_of(pieces, count):
    r = iota((count, PORTS), 0)
    out = jnp.zeros((count, PORTS), F32)
    for k, piece in enumerate(pieces):
        out = jnp.where(r == k, piece, out)
    return out.astype(BF16)


def own_lanes():
    own = lax.axis_index("owner")
    return iota((OWN, PORTS), 1) == own * OWN + iota((OWN, PORTS), 0)


def label_kernel(off_ref, diag_ref, z_ref):
    z_ref[:OWN, :] = off_ref[...]
    diag = jnp.sum(jnp.where(iota((OWN, OWN), 0) == iota((OWN, OWN), 1), diag_ref[...], 0.0), axis=1, keepdims=True)
    placed = jnp.sum(jnp.where(own_lanes(), diag, 0.0), axis=0, keepdims=True)
    z_ref[OWN:, :] = rows_of(split(placed, 3), DROWS)


def label(off, diag):
    return pl.pallas_call(
        label_kernel,
        out_shape=jax.ShapeDtypeStruct((ZROWS, PORTS), BF16),
        compiler_params=params(),
        cost_estimate=cost(OWN * PORTS, 1 << 17),
        name="label",
    )(hbm(off), hbm(diag))


def prep_kernel(
    owner_ref, half_ref, port_ref, rows_ref, out_ref, target_ref, names, rows, stim, made, in_sems, out_sems
):
    small = [
        pltpu.make_async_copy(ref, names.at[k], in_sems.at[2 + k]) for k, ref in enumerate((owner_ref, half_ref, port_ref))
    ]
    for copy in small:
        copy.start()
    half_rows = ROWS // 2
    loads = [
        pltpu.make_async_copy(rows_ref.at[r : r + half_rows], rows.at[r : r + half_rows], in_sems.at[k])
        for k, r in enumerate(range(0, ROWS, half_rows))
    ]
    for load in loads:
        load.start()
    for copy in small:
        copy.wait()
    owner = names[0]
    named = iota((OWNERS, ROWS), 0) == owner
    earlier = jnp.where(iota((ROWS, ROWS), 0) < iota((ROWS, ROWS), 1), 1.0, 0.0).astype(BF16)
    before = jnp.dot(jnp.where(named, 1.0, 0.0).astype(BF16), earlier, preferred_element_type=F32)
    rank = jnp.sum(jnp.where(named, before, 0.0), axis=0, keepdims=True)
    target = owner * CAP + rank.astype(I32)
    target_ref[...] = target + SLOTS * names[1]
    scale = jnp.where(names[1] == 1, HALF_SCALE, 1.0)
    port = jnp.transpose(jnp.broadcast_to(names[2], (128, ROWS)))
    for k, load in enumerate(loads):
        load.wait()
        at = slice(k * half_rows, (k + 1) * half_rows)
        for j in range(0, PORTS, 128):
            lanes = slice(j, j + 128)
            bump = jnp.where(iota((half_rows, 128), 1) + j == port[at], 8.0, 0.0)
            stim[at, lanes] = (rows[at, lanes].astype(F32) + bump).astype(BF16)
    stores = []
    tile = 256
    for k, u in enumerate(range(0, SLOTS, tile)):
        route = jnp.where(iota((tile, ROWS), 0) + u == target, scale, 0.0).astype(BF16)
        made[u : u + tile, :] = jnp.dot(route, stim[...], preferred_element_type=F32).astype(BF16)
        store = pltpu.make_async_copy(made.at[u : u + tile], out_ref.at[u : u + tile], out_sems.at[k])
        store.start()
        stores.append(store)
    for store in stores:
        store.wait()


def prep(owner, half, port, rows):
    return pl.pallas_call(
        prep_kernel,
        in_specs=[ANYWHERE] * 4,
        out_specs=[ANYWHERE, IN_VMEM],
        out_shape=[pltpu.HBM((SLOTS, PORTS), BF16), jax.ShapeDtypeStruct((1, ROWS), I32)],
        scratch_shapes=[
            pltpu.VMEM((3, 1, ROWS), I32),
            pltpu.VMEM((ROWS, PORTS), BF16),
            pltpu.VMEM((ROWS, PORTS), BF16),
            pltpu.VMEM((SLOTS, PORTS), BF16),
            pltpu.SemaphoreType.DMA((5,)),
            pltpu.SemaphoreType.DMA((4,)),
        ],
        compiler_params=params(),
        cost_estimate=cost(2 * SLOTS * ROWS * PORTS, 4 << 20),
        name="prep",
    )(hbm(owner), hbm(half), hbm(port), hbm(rows))


def maps_kernel(x_ref, maps_ref, out_ref, maps, first, other, total, made, in_sems, out_sems):
    tile = 256
    tiles = SLOTS // tile
    loads = [
        pltpu.make_async_copy(maps_ref.at[h, r : r + tile], maps.at[h, r : r + tile], in_sems.at[h, k])
        for h in range(2)
        for k, r in enumerate(range(0, PORTS, tile))
    ]
    for load in loads[:tiles]:
        load.start()
    for r in range(0, SLOTS, tile):
        x = x_ref[r : r + tile, :]
        peak = jnp.abs(x[:, :128])
        for j in range(128, PORTS, 128):
            peak = jnp.maximum(peak, jnp.abs(x[:, j : j + 128]))
        second = jnp.max(peak.astype(F32), axis=1, keepdims=True) > HALF_MARK
        keep = jnp.where(second, 0.0, 1.0).astype(BF16)
        kept = x * keep
        first[r : r + tile, :] = kept
        other[r : r + tile, :] = x - kept
    for load in loads[tiles:]:
        load.start()
    for load in loads[:tiles]:
        load.wait()
    for n in range(0, PORTS, tile):
        total[:, n : n + tile] = jnp.dot(first[...], maps[0, :, n : n + tile], preferred_element_type=F32)
    for load in loads[tiles:]:
        load.wait()
    stores = []
    for k, r in enumerate(range(0, SLOTS, tile)):
        at = slice(r, r + tile)
        made[at, :] = (total[at, :] + jnp.dot(other[at, :], maps[1], preferred_element_type=F32)).astype(BF16)
        store = pltpu.make_async_copy(made.at[at], out_ref.at[at], out_sems.at[k])
        store.start()
        stores.append(store)
    for store in stores:
        store.wait()


def apply_maps(x, maps):
    return pl.pallas_call(
        maps_kernel,
        in_specs=[IN_VMEM, ANYWHERE],
        out_specs=ANYWHERE,
        out_shape=pltpu.HBM((SLOTS, PORTS), BF16),
        scratch_shapes=[
            pltpu.VMEM((2, PORTS, PORTS), BF16),
            pltpu.VMEM((SLOTS, PORTS), BF16),
            pltpu.VMEM((SLOTS, PORTS), BF16),
            pltpu.VMEM((SLOTS, PORTS), F32),
            pltpu.VMEM((SLOTS, PORTS), BF16),
            pltpu.SemaphoreType.DMA((2, 4)),
            pltpu.SemaphoreType.DMA((4,)),
        ],
        compiler_params=params(60),
        cost_estimate=cost(4 * SLOTS * PORTS * PORTS, 8 << 20),
        name="apply_maps",
    )(vmem(x), hbm(maps))


def permuted(values, order):
    out = jnp.zeros(values.shape, F32)
    for j in range(0, PORTS, 256):
        pick = jnp.where(iota((256, PORTS), 0) + j == order, 1.0, 0.0).astype(BF16)
        out = out + jnp.dot(values[:, j : j + 256], pick, preferred_element_type=F32)
    return out


def read_diag(z_ref):
    z = z_ref[OWN:, :].astype(F32)
    return z[0:1] + z[1:2] + z[2:3]


def column(placed):
    return jnp.sum(jnp.where(own_lanes(), placed, 0.0), axis=1, keepdims=True)


def inverse(placed):
    held = placed > 0.0
    return jnp.where(held, 1.0 / jnp.where(held, placed, 1.0), 0.0)


def low_levels_kernel(z0_ref, z1_ref, z2_ref, z3_ref, order_ref, z_ref, off_ref, diag_ref, gb_ref):
    picked = permuted(jnp.concatenate([z1_ref[:OWN, :], z3_ref[:OWN, :]], axis=0), order_ref[0:1, :])
    off1 = z0_ref[:OWN, :].astype(F32) + picked[:OWN]
    picked2 = permuted(jnp.concatenate([z2_ref[:OWN, :], picked[OWN:].astype(BF16)], axis=0), order_ref[1:2, :])
    off2 = off1 + (picked2[:OWN] + picked2[OWN:])
    d0 = read_diag(z0_ref)
    d1 = d0 + read_diag(z1_ref)
    d2 = d1 + (read_diag(z2_ref) + read_diag(z3_ref))
    z_ref[:OWN, :] = off2.astype(BF16)
    z_ref[OWN:, :] = rows_of(split(d2, 3), DROWS)
    off_ref[...] = off2
    r = iota((DROWS, PORTS), 0)
    diag_ref[...] = jnp.where(r == 0, d0, jnp.where(r == 1, d2, 0.0))
    gb_ref[:OWN, :] = ((jnp.where(own_lanes(), d0, 0.0) - off1) / column(d1)).astype(BF16)
    gb_ref[OWN:, :] = (off2 / column(d2)).astype(BF16)


def low_levels(z0, z1, z2, z3, order):
    return pl.pallas_call(
        low_levels_kernel,
        out_shape=[
            jax.ShapeDtypeStruct((ZROWS, PORTS), BF16),
            jax.ShapeDtypeStruct((OWN, PORTS), F32),
            jax.ShapeDtypeStruct((DROWS, PORTS), F32),
            jax.ShapeDtypeStruct((2 * OWN, PORTS), BF16),
        ],
        compiler_params=params(),
        cost_estimate=cost(4 * 64 * PORTS * PORTS, 1 << 20),
        name="low_levels",
    )(z0, z1, z2, z3, order)


def top_level_kernel(z4_ref, off_ref, diag_ref, gb_ref, order_ref, pack_ref):
    off3 = off_ref[...] + permuted(z4_ref[:OWN, :], order_ref[2:3, :])
    d0, d2 = diag_ref[0:1, :], diag_ref[1:2, :]
    d3 = d2 + read_diag(z4_ref)
    pack_ref[: 2 * OWN, :] = gb_ref[...]
    pack_ref[2 * OWN : 3 * OWN, :] = (off3 / column(d3)).astype(BF16)
    pieces = split(inverse(d0), 3) + split(inverse(d3), 3) + split(d0 * inverse(d2), 2)
    pack_ref[3 * OWN :, :] = rows_of(pieces, DROWS)


def top_level(z4, off, diag, gb, order):
    return pl.pallas_call(
        top_level_kernel,
        out_shape=jax.ShapeDtypeStruct((PACK, PORTS), BF16),
        compiler_params=params(),
        cost_estimate=cost(2 * 32 * PORTS * PORTS, 1 << 20),
        name="top_level",
    )(z4, off, diag, gb, order)


def row_starts(side, lines):
    own = lax.axis_index("owner")
    core, x, y = own & 1, (own >> 1) & 3, own >> 3
    c = core if side == 0 else 1 - core
    starts = []
    for away, blocks in lines:
        for k in blocks:
            dx = jnp.where(c == 0, NEAR[k], away)
            dy = jnp.where(c == 0, away, NEAR[k])
            start = ((((y + dy) & 3) * 4 + ((x + dx) & 3)) * 2 + c) * OWN
            starts.append(pl.multiple_of(start, OWN))
    return starts


def arrange_kernel(*refs):
    parts, (held_ref, diag_ref, marks, sems) = refs[:6], refs[6:]
    copies = []
    for side in range(2):
        for n, start in enumerate(row_starts(side, NEAR_LINES)):
            block = parts[3 * side + n // 4].at[n % 4]
            for j in range(3):
                copies.append(
                    pltpu.make_async_copy(
                        block.at[j * OWN : (j + 1) * OWN], held_ref.at[j, pl.ds(start, OWN), :], sems.at[j]
                    )
                )
            copies.append(pltpu.make_async_copy(block.at[3 * OWN :], marks.at[12 * side + n], sems.at[3]))
    for copy in copies:
        copy.start()
    for copy in copies:
        copy.wait()
    diag_ref[...] = jnp.sum(marks[...].astype(F32), axis=0)


def arrange(parts):
    return pl.pallas_call(
        arrange_kernel,
        in_specs=[ANYWHERE] * 6,
        out_specs=[ANYWHERE, IN_VMEM],
        out_shape=[pltpu.HBM((3, PORTS, PORTS), BF16), pltpu.VMEM((DROWS, PORTS), F32)],
        scratch_shapes=[pltpu.VMEM((24, DROWS, PORTS), BF16), pltpu.SemaphoreType.DMA((4,))],
        compiler_params=params(),
        cost_estimate=cost(1 << 20, 11 << 20),
        name="arrange",
    )(*parts)


def finish_kernel(target_ref, ret_ref, diag_ref, held_ref, *refs):
    far_refs = refs[:4]
    out_ref, route, held, far, response, panel, made, held_sems, far_sems, out_sems = refs[4:]
    held_loads = [pltpu.make_async_copy(held_ref.at[j], held.at[j], held_sems.at[j]) for j in range(3)]
    far_loads = [pltpu.make_async_copy(far_refs[p], far.at[p], far_sems.at[p]) for p in range(4)]
    for load in held_loads[:1] + far_loads + held_loads[1:]:
        load.start()
    code = jnp.transpose(jnp.broadcast_to(target_ref[...], (128, ROWS)))
    scale = jnp.where(code >= SLOTS, 1.0 / HALF_SCALE, 1.0)
    target = code & (SLOTS - 1)
    for j in range(0, SLOTS, 128):
        route[:, j : j + 128] = jnp.where(iota((ROWS, 128), 1) + j == target, scale, 0.0).astype(BF16)
    wide = 256
    for n in range(0, PORTS, wide):
        at = slice(n, n + wide)
        response[:, at] = jnp.dot(route[...], ret_ref[:, at], preferred_element_type=F32)
    for load in far_loads:
        load.wait()
    total = diag_ref[...]
    for p in range(4):
        for k in range(2):
            total = total + far[p, k, 3 * OWN :, :].astype(F32)
    inv0 = total[0:1] + total[1:2] + total[2:3]
    inv3 = total[3:4] + total[4:5] + total[5:6]
    inv2 = inv0 * (total[6:7] + total[7:8])
    starts = [row_starts(side, FAR_LINES) for side in range(2)]

    def ready(level):
        held_loads[level].wait()
        for p in range(4):
            for k in range(2):
                at = pl.ds(starts[p // 2][2 * (p % 2) + k], OWN)
                held[level, at, :] = far[p, k, level * OWN : (level + 1) * OWN, :]

    panel[0] = (response[...] * inv0).astype(BF16)
    ready(0)
    for n in range(0, PORTS, wide):
        at = slice(n, n + wide)
        panel[1, :, at] = across(panel[0], held[0, at, :]).astype(BF16)
    ready(1)
    for n in range(0, PORTS, wide):
        at = slice(n, n + wide)
        panel[0, :, at] = (response[:, at] * inv2[:, at] - across(panel[1], held[1, at, :])).astype(BF16)
    ready(2)
    stores = []
    tile = 256
    for k, r in enumerate(range(0, ROWS, tile)):
        at = slice(r, r + tile)
        made[at, :] = response[at, :] * inv3 - across(panel[0, at, :], held[2])
        store = pltpu.make_async_copy(made.at[at], out_ref.at[at], out_sems.at[k])
        store.start()
        stores.append(store)
    for store in stores:
        store.wait()


def across(rows, matrix):
    return lax.dot_general(rows, matrix, (((1,), (1,)), ((), ())), preferred_element_type=F32)


def finish(target, returned, diag, held, far):
    return pl.pallas_call(
        finish_kernel,
        in_specs=[IN_VMEM] * 3 + [ANYWHERE] * 5,
        out_specs=ANYWHERE,
        out_shape=pltpu.HBM((ROWS, PORTS), F32),
        scratch_shapes=[
            pltpu.VMEM((ROWS, SLOTS), BF16),
            pltpu.VMEM((3, PORTS, PORTS), BF16),
            pltpu.VMEM((4, 2, PACK, PORTS), BF16),
            pltpu.VMEM((ROWS, PORTS), F32),
            pltpu.VMEM((2, ROWS, PORTS), BF16),
            pltpu.VMEM((ROWS, PORTS), F32),
            pltpu.SemaphoreType.DMA((3,)),
            pltpu.SemaphoreType.DMA((4,)),
            pltpu.SemaphoreType.DMA((2,)),
        ],
        compiler_params=params(28),
        cost_estimate=cost(8 * ROWS * PORTS * PORTS, 12 << 20),
        name="finish",
    )(vmem(target), vmem(returned), vmem(diag), hbm(held), *far)


def group_swap(value, mask):
    return lax.ppermute(value, "group", [(i, i ^ mask) for i in range(8)])


def chip_shift(value, step, turn):
    pairs = []
    for o in range(OWNERS):
        c, x, y = o & 1, (o >> 1) & 3, o >> 3
        if (c ^ turn) == 0:
            x = (x + step) % 4
        else:
            y = (y + step) % 4
        pairs.append((o, (y * 4 + x) * 2 + c))
    return lax.ppermute(value, "owner", pairs)


def core_swap(value):
    return lax.ppermute(value, "owner", [(o, o ^ 1) for o in range(OWNERS)])


def exchange(value):
    shape = value.shape
    value = value.reshape(OWNERS, CAP, PORTS)
    return lax.all_to_all(value, "owner", split_axis=0, concat_axis=0, tiled=True).reshape(shape)


def body(port_rows, defect_owner, defect_half, defect_port, subcircuit_maps, schur_off, schur_diag, pivot_order):
    z0 = label(schur_off, schur_diag.reshape(1, OWN))
    z1, z2, z3 = (group_swap(z0, mask) for mask in (1, 2, 3))
    outgoing, target = prep(
        defect_owner.reshape(1, ROWS), defect_half.reshape(1, ROWS), defect_port.reshape(1, ROWS), port_rows
    )
    arrived = exchange(outgoing)
    z, off, diag, gb = low_levels(z0, z1, z2, z3, pivot_order)
    pack = top_level(group_swap(z, 4), off, diag, gb, pivot_order)
    line = jnp.stack([pack] + [chip_shift(pack, step, 0) for step in STEPS])
    line, arrived = lax.optimization_barrier((line, arrived))
    left, right = chip_shift(line, 1, 1), chip_shift(line, -1, 1)
    answers = apply_maps(arrived, subcircuit_maps)
    answers, left, right = lax.optimization_barrier((answers, left, right))
    far_low, far_high = chip_shift(left[:2], 1, 1), chip_shift(right[2:], -1, 1)
    near = [line, left, right]
    held, diag_sum = arrange(near + [core_swap(part) for part in near])
    returned = exchange(answers)
    far_low, far_high, held, returned = lax.optimization_barrier((far_low, far_high, held, returned))
    far = [far_low, far_high, core_swap(far_low), core_swap(far_high)]
    return finish(target, returned, diag_sum, held, far)


def solution(mesh):
    return jax.shard_map(
        body,
        mesh=mesh,
        in_specs=(
            P(("group", "owner"), None),
            P(("group", "owner"), None),
            P(("group", "owner")),
            P(("group", "owner")),
            P(("group", "owner"), None, None),
            P(("group", "owner"), None),
            P(("group", "owner")),
            P(),
        ),
        out_specs=P(("group", "owner"), None),
        check_vma=False,
    )
```

```python
import jax
import jax.numpy as jnp
from jax import lax
from jax.experimental import pallas as pl
from jax.experimental.pallas import tpu as pltpu
from jax.sharding import PartitionSpec as P

BF16 = jnp.bfloat16
F32 = jnp.float32
I32 = jnp.int32

ROWS = 512
PORTS = 1024
OWNERS = 32
CAP = 32
SLOTS = OWNERS * CAP
OWN = 32
DROWS = 8
ZROWS = OWN + DROWS
PACK = 3 * OWN + DROWS
HALF_SCALE = 64.0
HALF_MARK = 32.0
STEPS = (1, -1, 2)
NEAR = (0, -1, 1, -2)
LINES = ((0, 0), (-1, 0), (1, 0), (2, 0), (2, 2))


def iota(shape, dim):
    return lax.broadcasted_iota(I32, shape, dim)


def params(limit=20, dims=None):
    return pltpu.CompilerParams(vmem_limit_bytes=limit << 20, dimension_semantics=dims)


def cost(flops, nbytes):
    return pl.CostEstimate(flops=flops, bytes_accessed=nbytes, transcendentals=0)


def hbm(value):
    return pltpu.with_memory_space_constraint(value, pltpu.HBM)


def vmem(value):
    return pltpu.with_memory_space_constraint(value, pltpu.VMEM)


ANYWHERE = pl.BlockSpec(memory_space=pl.ANY)
IN_VMEM = pl.BlockSpec(memory_space=pltpu.VMEM)


def split(value, parts):
    pieces = []
    for _ in range(parts):
        piece = value.astype(BF16).astype(F32)
        pieces.append(piece)
        value = value - piece
    return pieces


def rows_of(pieces, count):
    r = iota((count, PORTS), 0)
    out = jnp.zeros((count, PORTS), F32)
    for k, piece in enumerate(pieces):
        out = jnp.where(r == k, piece, out)
    return out.astype(BF16)


def own_lanes():
    own = lax.axis_index("owner")
    return iota((OWN, PORTS), 1) == own * OWN + iota((OWN, PORTS), 0)


def label_kernel(off_ref, diag_ref, z_ref):
    z_ref[:OWN, :] = off_ref[...]
    diag = jnp.sum(jnp.where(iota((OWN, OWN), 0) == iota((OWN, OWN), 1), diag_ref[...], 0.0), axis=1, keepdims=True)
    placed = jnp.sum(jnp.where(own_lanes(), diag, 0.0), axis=0, keepdims=True)
    z_ref[OWN:, :] = rows_of(split(placed, 3), DROWS)


def label(off, diag):
    return pl.pallas_call(
        label_kernel,
        out_shape=jax.ShapeDtypeStruct((ZROWS, PORTS), BF16),
        compiler_params=params(),
        cost_estimate=cost(OWN * PORTS, 1 << 17),
        name="label",
    )(hbm(off), hbm(diag))


def prep_kernel(
    owner_ref, half_ref, port_ref, rows_ref, out_ref, target_ref, names, rows, stim, made, in_sems, out_sems
):
    small = [
        pltpu.make_async_copy(ref, names.at[k], in_sems.at[2 + k]) for k, ref in enumerate((owner_ref, half_ref, port_ref))
    ]
    for copy in small:
        copy.start()
    half_rows = ROWS // 2
    loads = [
        pltpu.make_async_copy(rows_ref.at[r : r + half_rows], rows.at[r : r + half_rows], in_sems.at[k])
        for k, r in enumerate(range(0, ROWS, half_rows))
    ]
    for load in loads:
        load.start()
    for copy in small:
        copy.wait()
    owner = names[0]
    named = iota((OWNERS, ROWS), 0) == owner
    earlier = jnp.where(iota((ROWS, ROWS), 0) < iota((ROWS, ROWS), 1), 1.0, 0.0).astype(BF16)
    before = jnp.dot(jnp.where(named, 1.0, 0.0).astype(BF16), earlier, preferred_element_type=F32)
    rank = jnp.sum(jnp.where(named, before, 0.0), axis=0, keepdims=True)
    target = owner * CAP + rank.astype(I32)
    target_ref[...] = target + SLOTS * names[1]
    scale = jnp.where(names[1] == 1, HALF_SCALE, 1.0)
    port = jnp.transpose(jnp.broadcast_to(names[2], (128, ROWS)))
    for k, load in enumerate(loads):
        load.wait()
        at = slice(k * half_rows, (k + 1) * half_rows)
        for j in range(0, PORTS, 128):
            lanes = slice(j, j + 128)
            bump = jnp.where(iota((half_rows, 128), 1) + j == port[at], 8.0, 0.0)
            stim[at, lanes] = (rows[at, lanes].astype(F32) + bump).astype(BF16)
    stores = []
    tile = 256
    for k, u in enumerate(range(0, SLOTS, tile)):
        route = jnp.where(iota((tile, ROWS), 0) + u == target, scale, 0.0).astype(BF16)
        made[u : u + tile, :] = jnp.dot(route, stim[...], preferred_element_type=F32).astype(BF16)
        store = pltpu.make_async_copy(made.at[u : u + tile], out_ref.at[u : u + tile], out_sems.at[k])
        store.start()
        stores.append(store)
    for store in stores:
        store.wait()


def prep(owner, half, port, rows):
    return pl.pallas_call(
        prep_kernel,
        in_specs=[ANYWHERE] * 4,
        out_specs=[ANYWHERE, IN_VMEM],
        out_shape=[pltpu.HBM((SLOTS, PORTS), BF16), jax.ShapeDtypeStruct((1, ROWS), I32)],
        scratch_shapes=[
            pltpu.VMEM((3, 1, ROWS), I32),
            pltpu.VMEM((ROWS, PORTS), BF16),
            pltpu.VMEM((ROWS, PORTS), BF16),
            pltpu.VMEM((SLOTS, PORTS), BF16),
            pltpu.SemaphoreType.DMA((5,)),
            pltpu.SemaphoreType.DMA((4,)),
        ],
        compiler_params=params(),
        cost_estimate=cost(2 * SLOTS * ROWS * PORTS, 4 << 20),
        name="prep",
    )(hbm(owner), hbm(half), hbm(port), hbm(rows))


def maps_kernel(x_ref, maps_ref, out_ref, maps, first, other, total, made, in_sems, out_sems):
    tile = 256
    tiles = SLOTS // tile
    loads = [
        pltpu.make_async_copy(maps_ref.at[h, r : r + tile], maps.at[h, r : r + tile], in_sems.at[h, k])
        for h in range(2)
        for k, r in enumerate(range(0, PORTS, tile))
    ]
    for load in loads[:tiles]:
        load.start()
    for r in range(0, SLOTS, tile):
        x = x_ref[r : r + tile, :]
        peak = jnp.abs(x[:, :128])
        for j in range(128, PORTS, 128):
            peak = jnp.maximum(peak, jnp.abs(x[:, j : j + 128]))
        second = jnp.max(peak.astype(F32), axis=1, keepdims=True) > HALF_MARK
        keep = jnp.where(second, 0.0, 1.0).astype(BF16)
        kept = x * keep
        first[r : r + tile, :] = kept
        other[r : r + tile, :] = x - kept
    for load in loads[tiles:]:
        load.start()
    for load in loads[:tiles]:
        load.wait()
    for n in range(0, PORTS, tile):
        total[:, n : n + tile] = jnp.dot(first[...], maps[0, :, n : n + tile], preferred_element_type=F32)
    for load in loads[tiles:]:
        load.wait()
    stores = []
    for k, r in enumerate(range(0, SLOTS, tile)):
        at = slice(r, r + tile)
        made[at, :] = (total[at, :] + jnp.dot(other[at, :], maps[1], preferred_element_type=F32)).astype(BF16)
        store = pltpu.make_async_copy(made.at[at], out_ref.at[at], out_sems.at[k])
        store.start()
        stores.append(store)
    for store in stores:
        store.wait()


def apply_maps(x, maps):
    return pl.pallas_call(
        maps_kernel,
        in_specs=[IN_VMEM, ANYWHERE],
        out_specs=ANYWHERE,
        out_shape=pltpu.HBM((SLOTS, PORTS), BF16),
        scratch_shapes=[
            pltpu.VMEM((2, PORTS, PORTS), BF16),
            pltpu.VMEM((SLOTS, PORTS), BF16),
            pltpu.VMEM((SLOTS, PORTS), BF16),
            pltpu.VMEM((SLOTS, PORTS), F32),
            pltpu.VMEM((SLOTS, PORTS), BF16),
            pltpu.SemaphoreType.DMA((2, 4)),
            pltpu.SemaphoreType.DMA((4,)),
        ],
        compiler_params=params(28),
        cost_estimate=cost(4 * SLOTS * PORTS * PORTS, 8 << 20),
        name="apply_maps",
    )(vmem(x), hbm(maps))


def permuted(values, order):
    out = jnp.zeros(values.shape, F32)
    for j in range(0, PORTS, 256):
        pick = jnp.where(iota((256, PORTS), 0) + j == order, 1.0, 0.0).astype(BF16)
        out = out + jnp.dot(values[:, j : j + 256], pick, preferred_element_type=F32)
    return out


def read_diag(z_ref):
    z = z_ref[OWN:, :].astype(F32)
    return z[0:1] + z[1:2] + z[2:3]


def column(placed):
    return jnp.sum(jnp.where(own_lanes(), placed, 0.0), axis=1, keepdims=True)


def inverse(placed):
    held = placed > 0.0
    return jnp.where(held, 1.0 / jnp.where(held, placed, 1.0), 0.0)


def low_levels_kernel(z0_ref, z1_ref, z2_ref, z3_ref, order_ref, z_ref, off_ref, diag_ref, gb_ref):
    picked = permuted(jnp.concatenate([z1_ref[:OWN, :], z3_ref[:OWN, :]], axis=0), order_ref[0:1, :])
    off1 = z0_ref[:OWN, :].astype(F32) + picked[:OWN]
    picked2 = permuted(jnp.concatenate([z2_ref[:OWN, :], picked[OWN:].astype(BF16)], axis=0), order_ref[1:2, :])
    off2 = off1 + (picked2[:OWN] + picked2[OWN:])
    d0 = read_diag(z0_ref)
    d1 = d0 + read_diag(z1_ref)
    d2 = d1 + (read_diag(z2_ref) + read_diag(z3_ref))
    z_ref[:OWN, :] = off2.astype(BF16)
    z_ref[OWN:, :] = rows_of(split(d2, 3), DROWS)
    off_ref[...] = off2
    r = iota((DROWS, PORTS), 0)
    diag_ref[...] = jnp.where(r == 0, d0, jnp.where(r == 1, d2, 0.0))
    gb_ref[:OWN, :] = ((jnp.where(own_lanes(), d0, 0.0) - off1) / column(d1)).astype(BF16)
    gb_ref[OWN:, :] = (off2 / column(d2)).astype(BF16)


def low_levels(z0, z1, z2, z3, order):
    return pl.pallas_call(
        low_levels_kernel,
        out_shape=[
            jax.ShapeDtypeStruct((ZROWS, PORTS), BF16),
            jax.ShapeDtypeStruct((OWN, PORTS), F32),
            jax.ShapeDtypeStruct((DROWS, PORTS), F32),
            jax.ShapeDtypeStruct((2 * OWN, PORTS), BF16),
        ],
        compiler_params=params(),
        cost_estimate=cost(4 * 64 * PORTS * PORTS, 1 << 20),
        name="low_levels",
    )(z0, z1, z2, z3, order)


def top_level_kernel(z4_ref, off_ref, diag_ref, gb_ref, order_ref, pack_ref):
    off3 = off_ref[...] + permuted(z4_ref[:OWN, :], order_ref[2:3, :])
    d0, d2 = diag_ref[0:1, :], diag_ref[1:2, :]
    d3 = d2 + read_diag(z4_ref)
    pack_ref[: 2 * OWN, :] = gb_ref[...]
    pack_ref[2 * OWN : 3 * OWN, :] = (off3 / column(d3)).astype(BF16)
    pieces = split(inverse(d0), 3) + split(inverse(d3), 3) + split(d0 * inverse(d2), 2)
    pack_ref[3 * OWN :, :] = rows_of(pieces, DROWS)


def top_level(z4, off, diag, gb, order):
    return pl.pallas_call(
        top_level_kernel,
        out_shape=jax.ShapeDtypeStruct((PACK, PORTS), BF16),
        compiler_params=params(),
        cost_estimate=cost(2 * 32 * PORTS * PORTS, 1 << 20),
        name="top_level",
    )(z4, off, diag, gb, order)


def fold_kernel(*refs):
    parts, (f_ref, diag_ref, held, marks, mid, made, sems) = refs[: 2 * len(LINES)], refs[2 * len(LINES) :]
    own = lax.axis_index("owner")
    core, x, y = own & 1, (own >> 1) & 3, own >> 3
    slot = 0
    for side in range(2):
        c = core if side == 0 else 1 - core
        for m, (away, first) in enumerate(LINES):
            for k in range(parts[side * len(LINES) + m].shape[0]):
                dx = jnp.where(c == 0, NEAR[k + first], away)
                dy = jnp.where(c == 0, away, NEAR[k + first])
                start = ((((y + dy) & 3) * 4 + ((x + dx) & 3)) * 2 + c) * OWN
                at = pl.ds(pl.multiple_of(start, OWN), OWN)
                block = parts[side * len(LINES) + m]
                for j in range(3):
                    held[j, at, :] = block[k, j * OWN : (j + 1) * OWN, :]
                marks[slot] = block[k, 3 * OWN :, :]
                slot += 1
    total = jnp.sum(marks[...].astype(F32), axis=0)
    inv0 = total[0:1] + total[1:2] + total[2:3]
    inv3 = total[3:4] + total[4:5] + total[5:6]
    ratio = total[6:7] + total[7:8]
    r = iota((DROWS, PORTS), 0)
    diag_ref[...] = jnp.where(r == 0, inv0, jnp.where(r == 1, inv3, 0.0))
    tile = 256
    for t in range(0, PORTS, tile):
        acc = jnp.dot(held[1], held[0, :, t : t + tile], preferred_element_type=F32)
        on = iota((PORTS, tile), 0) == iota((PORTS, tile), 1) + t
        mid[:, t : t + tile] = (jnp.where(on, ratio[:, t : t + tile], 0.0) - acc).astype(BF16)
    stores = []
    for k, t in enumerate(range(0, PORTS, tile)):
        at = slice(t, t + tile)
        made[at, :] = jnp.dot(held[2, at, :], mid[...], preferred_element_type=F32).astype(BF16)
        store = pltpu.make_async_copy(made.at[at], f_ref.at[at], sems.at[k])
        store.start()
        stores.append(store)
    for store in stores:
        store.wait()


def fold(parts):
    return pl.pallas_call(
        fold_kernel,
        in_specs=[IN_VMEM] * (2 * len(LINES)),
        out_specs=[ANYWHERE, IN_VMEM],
        out_shape=[pltpu.HBM((PORTS, PORTS), BF16), pltpu.VMEM((DROWS, PORTS), F32)],
        scratch_shapes=[
            pltpu.VMEM((3, PORTS, PORTS), BF16),
            pltpu.VMEM((32, DROWS, PORTS), BF16),
            pltpu.VMEM((PORTS, PORTS), BF16),
            pltpu.VMEM((PORTS, PORTS), BF16),
            pltpu.SemaphoreType.DMA((4,)),
        ],
        compiler_params=params(24),
        cost_estimate=cost(4 * PORTS**3, 9 << 20),
        name="fold",
    )(*[vmem(part) for part in parts])


def finish_kernel(target_ref, ret_ref, f_ref, diag_ref, out_ref, route, response, scaled, coupling, made, in_sem, out_sems):
    load = pltpu.make_async_copy(f_ref, coupling, in_sem)
    load.start()
    code = jnp.transpose(jnp.broadcast_to(target_ref[...], (128, ROWS)))
    scale = jnp.where(code >= SLOTS, 1.0 / HALF_SCALE, 1.0)
    target = code & (SLOTS - 1)
    for j in range(0, SLOTS, 128):
        route[:, j : j + 128] = jnp.where(iota((ROWS, 128), 1) + j == target, scale, 0.0).astype(BF16)
    for n in range(0, PORTS, 256):
        at = slice(n, n + 256)
        piece = jnp.dot(route[...], ret_ref[:, at], preferred_element_type=F32)
        response[:, at] = piece
        scaled[:, at] = (piece * diag_ref[0:1, at]).astype(BF16)
    load.wait()
    stores = []
    tile = 256
    for k, n in enumerate(range(0, PORTS, tile)):
        at = slice(n, n + tile)
        coupled = lax.dot_general(
            scaled[...], coupling[at, :], (((1,), (1,)), ((), ())), preferred_element_type=F32
        )
        made[:, at] = response[:, at] * diag_ref[1:2, at] - coupled
        store = pltpu.make_async_copy(made.at[:, at], out_ref.at[:, at], out_sems.at[k])
        store.start()
        stores.append(store)
    for store in stores:
        store.wait()


def finish(target, returned, f, diag):
    return pl.pallas_call(
        finish_kernel,
        in_specs=[IN_VMEM, IN_VMEM, ANYWHERE, IN_VMEM],
        out_specs=ANYWHERE,
        out_shape=pltpu.HBM((ROWS, PORTS), F32),
        scratch_shapes=[
            pltpu.VMEM((ROWS, SLOTS), BF16),
            pltpu.VMEM((ROWS, PORTS), F32),
            pltpu.VMEM((ROWS, PORTS), BF16),
            pltpu.VMEM((PORTS, PORTS), BF16),
            pltpu.VMEM((ROWS, PORTS), F32),
            pltpu.SemaphoreType.DMA,
            pltpu.SemaphoreType.DMA((4,)),
        ],
        compiler_params=params(24),
        cost_estimate=cost(4 * ROWS * PORTS * PORTS, 6 << 20),
        name="finish",
    )(vmem(target), vmem(returned), hbm(f), vmem(diag))


def group_swap(value, mask):
    return lax.ppermute(value, "group", [(i, i ^ mask) for i in range(8)])


def chip_shift(value, step, turn):
    pairs = []
    for o in range(OWNERS):
        c, x, y = o & 1, (o >> 1) & 3, o >> 3
        if (c ^ turn) == 0:
            x = (x + step) % 4
        else:
            y = (y + step) % 4
        pairs.append((o, (y * 4 + x) * 2 + c))
    return lax.ppermute(value, "owner", pairs)


def core_swap(value):
    return lax.ppermute(value, "owner", [(o, o ^ 1) for o in range(OWNERS)])


def exchange(value):
    shape = value.shape
    value = value.reshape(OWNERS, CAP, PORTS)
    return lax.all_to_all(value, "owner", split_axis=0, concat_axis=0, tiled=True).reshape(shape)


def body(port_rows, defect_owner, defect_half, defect_port, subcircuit_maps, schur_off, schur_diag, pivot_order):
    z0 = label(schur_off, schur_diag.reshape(1, OWN))
    z1, z2, z3 = (group_swap(z0, mask) for mask in (1, 2, 3))
    outgoing, target = prep(
        defect_owner.reshape(1, ROWS), defect_half.reshape(1, ROWS), defect_port.reshape(1, ROWS), port_rows
    )
    arrived = exchange(outgoing)
    z, off, diag, gb = low_levels(z0, z1, z2, z3, pivot_order)
    pack = top_level(group_swap(z, 4), off, diag, gb, pivot_order)
    line = jnp.stack([pack] + [chip_shift(pack, step, 0) for step in STEPS])
    left, right = chip_shift(line, 1, 1), chip_shift(line, -1, 1)
    far_low, far_high = chip_shift(left[:2], 1, 1), chip_shift(right[2:], -1, 1)
    parts = [line, left, right, far_low, far_high]
    parts = parts + [core_swap(part) for part in parts]
    f, inverses = fold(parts)
    answers = apply_maps(arrived, subcircuit_maps)
    returned = exchange(answers)
    return finish(target, returned, f, inverses)


def solution(mesh):
    return jax.shard_map(
        body,
        mesh=mesh,
        in_specs=(
            P(("group", "owner"), None),
            P(("group", "owner"), None),
            P(("group", "owner")),
            P(("group", "owner")),
            P(("group", "owner"), None, None),
            P(("group", "owner"), None),
            P(("group", "owner")),
            P(),
        ),
        out_specs=P(("group", "owner"), None),
        check_vma=False,
    )
```

```python
import jax
import jax.numpy as jnp
from jax import lax
from jax.experimental import pallas as pl
from jax.experimental.pallas import tpu as pltpu
from jax.sharding import PartitionSpec as P

BF16 = jnp.bfloat16
F32 = jnp.float32
I32 = jnp.int32

ROWS = 512
PORTS = 1024
OWNERS = 32
CAP = 32
SLOTS = OWNERS * CAP
OWN = 32
DROWS = 8
ZROWS = OWN + DROWS
PACK = 3 * OWN + DROWS
HALF_SCALE = 64.0
HALF_MARK = 32.0
STEPS = (1, -1, 2)
NEAR = (0, -1, 1, -2)
LINES = ((0, 0), (-1, 0), (1, 0), (2, 0), (2, 2))


def iota(shape, dim):
    return lax.broadcasted_iota(I32, shape, dim)


def params(limit=20, dims=None):
    return pltpu.CompilerParams(vmem_limit_bytes=limit << 20, dimension_semantics=dims)


def cost(flops, nbytes):
    return pl.CostEstimate(flops=flops, bytes_accessed=nbytes, transcendentals=0)


def hbm(value):
    return pltpu.with_memory_space_constraint(value, pltpu.HBM)


def vmem(value):
    return pltpu.with_memory_space_constraint(value, pltpu.VMEM)


ANYWHERE = pl.BlockSpec(memory_space=pl.ANY)
IN_VMEM = pl.BlockSpec(memory_space=pltpu.VMEM)


def split(value, parts):
    pieces = []
    for _ in range(parts):
        piece = value.astype(BF16).astype(F32)
        pieces.append(piece)
        value = value - piece
    return pieces


def rows_of(pieces, count):
    r = iota((count, PORTS), 0)
    out = jnp.zeros((count, PORTS), F32)
    for k, piece in enumerate(pieces):
        out = jnp.where(r == k, piece, out)
    return out.astype(BF16)


def own_lanes():
    own = lax.axis_index("owner")
    return iota((OWN, PORTS), 1) == own * OWN + iota((OWN, PORTS), 0)


def label_kernel(off_ref, diag_ref, z_ref):
    z_ref[:OWN, :] = off_ref[...]
    diag = jnp.sum(jnp.where(iota((OWN, OWN), 0) == iota((OWN, OWN), 1), diag_ref[...], 0.0), axis=1, keepdims=True)
    placed = jnp.sum(jnp.where(own_lanes(), diag, 0.0), axis=0, keepdims=True)
    z_ref[OWN:, :] = rows_of(split(placed, 3), DROWS)


def label(off, diag):
    return pl.pallas_call(
        label_kernel,
        out_shape=jax.ShapeDtypeStruct((ZROWS, PORTS), BF16),
        compiler_params=params(),
        cost_estimate=cost(OWN * PORTS, 1 << 17),
        name="label",
    )(hbm(off), hbm(diag))


def prep_kernel(
    owner_ref, half_ref, port_ref, rows_ref, out_ref, target_ref, names, rows, stim, made, in_sems, out_sems
):
    small = [
        pltpu.make_async_copy(ref, names.at[k], in_sems.at[2 + k]) for k, ref in enumerate((owner_ref, half_ref, port_ref))
    ]
    for copy in small:
        copy.start()
    half_rows = ROWS // 2
    loads = [
        pltpu.make_async_copy(rows_ref.at[r : r + half_rows], rows.at[r : r + half_rows], in_sems.at[k])
        for k, r in enumerate(range(0, ROWS, half_rows))
    ]
    for load in loads:
        load.start()
    for copy in small:
        copy.wait()
    owner = names[0]
    named = iota((OWNERS, ROWS), 0) == owner
    earlier = jnp.where(iota((ROWS, ROWS), 0) < iota((ROWS, ROWS), 1), 1.0, 0.0).astype(BF16)
    before = jnp.dot(jnp.where(named, 1.0, 0.0).astype(BF16), earlier, preferred_element_type=F32)
    rank = jnp.sum(jnp.where(named, before, 0.0), axis=0, keepdims=True)
    target = owner * CAP + rank.astype(I32)
    target_ref[...] = target + SLOTS * names[1]
    scale = jnp.where(names[1] == 1, HALF_SCALE, 1.0)
    port = jnp.transpose(jnp.broadcast_to(names[2], (128, ROWS)))
    for k, load in enumerate(loads):
        load.wait()
        at = slice(k * half_rows, (k + 1) * half_rows)
        for j in range(0, PORTS, 128):
            lanes = slice(j, j + 128)
            bump = jnp.where(iota((half_rows, 128), 1) + j == port[at], 8.0, 0.0)
            stim[at, lanes] = (rows[at, lanes].astype(F32) + bump).astype(BF16)
    stores = []
    tile = 256
    for k, u in enumerate(range(0, SLOTS, tile)):
        route = jnp.where(iota((tile, ROWS), 0) + u == target, scale, 0.0).astype(BF16)
        made[u : u + tile, :] = jnp.dot(route, stim[...], preferred_element_type=F32).astype(BF16)
        store = pltpu.make_async_copy(made.at[u : u + tile], out_ref.at[u : u + tile], out_sems.at[k])
        store.start()
        stores.append(store)
    for store in stores:
        store.wait()


def prep(owner, half, port, rows):
    return pl.pallas_call(
        prep_kernel,
        in_specs=[ANYWHERE] * 4,
        out_specs=[ANYWHERE, IN_VMEM],
        out_shape=[pltpu.HBM((SLOTS, PORTS), BF16), jax.ShapeDtypeStruct((1, ROWS), I32)],
        scratch_shapes=[
            pltpu.VMEM((3, 1, ROWS), I32),
            pltpu.VMEM((ROWS, PORTS), BF16),
            pltpu.VMEM((ROWS, PORTS), BF16),
            pltpu.VMEM((SLOTS, PORTS), BF16),
            pltpu.SemaphoreType.DMA((5,)),
            pltpu.SemaphoreType.DMA((4,)),
        ],
        compiler_params=params(),
        cost_estimate=cost(2 * SLOTS * ROWS * PORTS, 4 << 20),
        name="prep",
    )(hbm(owner), hbm(half), hbm(port), hbm(rows))


def maps_kernel(x_ref, maps_ref, out_ref, maps, first, other, total, made, in_sems, out_sems):
    tile = 256
    tiles = SLOTS // tile
    loads = [
        pltpu.make_async_copy(maps_ref.at[h, r : r + tile], maps.at[h, r : r + tile], in_sems.at[h, k])
        for h in range(2)
        for k, r in enumerate(range(0, PORTS, tile))
    ]
    for load in loads[:tiles]:
        load.start()
    for r in range(0, SLOTS, tile):
        x = x_ref[r : r + tile, :]
        peak = jnp.abs(x[:, :128])
        for j in range(128, PORTS, 128):
            peak = jnp.maximum(peak, jnp.abs(x[:, j : j + 128]))
        second = jnp.max(peak.astype(F32), axis=1, keepdims=True) > HALF_MARK
        keep = jnp.where(second, 0.0, 1.0).astype(BF16)
        kept = x * keep
        first[r : r + tile, :] = kept
        other[r : r + tile, :] = x - kept
    for load in loads[tiles:]:
        load.start()
    for load in loads[:tiles]:
        load.wait()
    for n in range(0, PORTS, tile):
        total[:, n : n + tile] = jnp.dot(first[...], maps[0, :, n : n + tile], preferred_element_type=F32)
    for load in loads[tiles:]:
        load.wait()
    stores = []
    for k, r in enumerate(range(0, SLOTS, tile)):
        at = slice(r, r + tile)
        made[at, :] = (total[at, :] + jnp.dot(other[at, :], maps[1], preferred_element_type=F32)).astype(BF16)
        store = pltpu.make_async_copy(made.at[at], out_ref.at[at], out_sems.at[k])
        store.start()
        stores.append(store)
    for store in stores:
        store.wait()


def apply_maps(x, maps):
    return pl.pallas_call(
        maps_kernel,
        in_specs=[IN_VMEM, ANYWHERE],
        out_specs=ANYWHERE,
        out_shape=pltpu.HBM((SLOTS, PORTS), BF16),
        scratch_shapes=[
            pltpu.VMEM((2, PORTS, PORTS), BF16),
            pltpu.VMEM((SLOTS, PORTS), BF16),
            pltpu.VMEM((SLOTS, PORTS), BF16),
            pltpu.VMEM((SLOTS, PORTS), F32),
            pltpu.VMEM((SLOTS, PORTS), BF16),
            pltpu.SemaphoreType.DMA((2, 4)),
            pltpu.SemaphoreType.DMA((4,)),
        ],
        compiler_params=params(60),
        cost_estimate=cost(4 * SLOTS * PORTS * PORTS, 8 << 20),
        name="apply_maps",
    )(vmem(x), hbm(maps))


def permuted(values, order):
    out = jnp.zeros(values.shape, F32)
    for j in range(0, PORTS, 256):
        pick = jnp.where(iota((256, PORTS), 0) + j == order, 1.0, 0.0).astype(BF16)
        out = out + jnp.dot(values[:, j : j + 256], pick, preferred_element_type=F32)
    return out


def read_diag(z_ref):
    z = z_ref[OWN:, :].astype(F32)
    return z[0:1] + z[1:2] + z[2:3]


def column(placed):
    return jnp.sum(jnp.where(own_lanes(), placed, 0.0), axis=1, keepdims=True)


def inverse(placed):
    held = placed > 0.0
    return jnp.where(held, 1.0 / jnp.where(held, placed, 1.0), 0.0)


def low_levels_kernel(z0_ref, z1_ref, z2_ref, z3_ref, order_ref, z_ref, off_ref, diag_ref, gb_ref):
    picked = permuted(jnp.concatenate([z1_ref[:OWN, :], z3_ref[:OWN, :]], axis=0), order_ref[0:1, :])
    off1 = z0_ref[:OWN, :].astype(F32) + picked[:OWN]
    picked2 = permuted(jnp.concatenate([z2_ref[:OWN, :], picked[OWN:].astype(BF16)], axis=0), order_ref[1:2, :])
    off2 = off1 + (picked2[:OWN] + picked2[OWN:])
    d0 = read_diag(z0_ref)
    d1 = d0 + read_diag(z1_ref)
    d2 = d1 + (read_diag(z2_ref) + read_diag(z3_ref))
    z_ref[:OWN, :] = off2.astype(BF16)
    z_ref[OWN:, :] = rows_of(split(d2, 3), DROWS)
    off_ref[...] = off2
    r = iota((DROWS, PORTS), 0)
    diag_ref[...] = jnp.where(r == 0, d0, jnp.where(r == 1, d2, 0.0))
    gb_ref[:OWN, :] = ((jnp.where(own_lanes(), d0, 0.0) - off1) / column(d1)).astype(BF16)
    gb_ref[OWN:, :] = (off2 / column(d2)).astype(BF16)


def low_levels(z0, z1, z2, z3, order):
    return pl.pallas_call(
        low_levels_kernel,
        out_shape=[
            jax.ShapeDtypeStruct((ZROWS, PORTS), BF16),
            jax.ShapeDtypeStruct((OWN, PORTS), F32),
            jax.ShapeDtypeStruct((DROWS, PORTS), F32),
            jax.ShapeDtypeStruct((2 * OWN, PORTS), BF16),
        ],
        compiler_params=params(),
        cost_estimate=cost(4 * 64 * PORTS * PORTS, 1 << 20),
        name="low_levels",
    )(z0, z1, z2, z3, order)


def top_level_kernel(z4_ref, off_ref, diag_ref, gb_ref, order_ref, pack_ref):
    off3 = off_ref[...] + permuted(z4_ref[:OWN, :], order_ref[2:3, :])
    d0, d2 = diag_ref[0:1, :], diag_ref[1:2, :]
    d3 = d2 + read_diag(z4_ref)
    pack_ref[: 2 * OWN, :] = gb_ref[...]
    pack_ref[2 * OWN : 3 * OWN, :] = (off3 / column(d3)).astype(BF16)
    pieces = split(inverse(d0), 3) + split(inverse(d3), 3) + split(d0 * inverse(d2), 2)
    pack_ref[3 * OWN :, :] = rows_of(pieces, DROWS)


def top_level(z4, off, diag, gb, order):
    return pl.pallas_call(
        top_level_kernel,
        out_shape=jax.ShapeDtypeStruct((PACK, PORTS), BF16),
        compiler_params=params(),
        cost_estimate=cost(2 * 32 * PORTS * PORTS, 1 << 20),
        name="top_level",
    )(z4, off, diag, gb, order)


def fold_kernel(*refs):
    parts, (f_ref, diag_ref, held, marks, mid, made, sems) = refs[: 2 * len(LINES)], refs[2 * len(LINES) :]
    own = lax.axis_index("owner")
    core, x, y = own & 1, (own >> 1) & 3, own >> 3
    slot = 0
    for side in range(2):
        c = core if side == 0 else 1 - core
        for m, (away, first) in enumerate(LINES):
            for k in range(parts[side * len(LINES) + m].shape[0]):
                dx = jnp.where(c == 0, NEAR[k + first], away)
                dy = jnp.where(c == 0, away, NEAR[k + first])
                start = ((((y + dy) & 3) * 4 + ((x + dx) & 3)) * 2 + c) * OWN
                at = pl.ds(pl.multiple_of(start, OWN), OWN)
                block = parts[side * len(LINES) + m]
                for j in range(3):
                    held[j, at, :] = block[k, j * OWN : (j + 1) * OWN, :]
                marks[slot] = block[k, 3 * OWN :, :]
                slot += 1
    total = jnp.sum(marks[...].astype(F32), axis=0)
    inv0 = total[0:1] + total[1:2] + total[2:3]
    inv3 = total[3:4] + total[4:5] + total[5:6]
    ratio = total[6:7] + total[7:8]
    r = iota((DROWS, PORTS), 0)
    diag_ref[...] = jnp.where(r == 0, inv0, jnp.where(r == 1, inv3, 0.0))
    tile = 256
    for t in range(0, PORTS, tile):
        acc = jnp.dot(held[1], held[0, :, t : t + tile], preferred_element_type=F32)
        on = iota((PORTS, tile), 0) == iota((PORTS, tile), 1) + t
        mid[:, t : t + tile] = (jnp.where(on, ratio[:, t : t + tile], 0.0) - acc).astype(BF16)
    stores = []
    for k, t in enumerate(range(0, PORTS, tile)):
        at = slice(t, t + tile)
        made[at, :] = jnp.dot(held[2, at, :], mid[...], preferred_element_type=F32).astype(BF16)
        store = pltpu.make_async_copy(made.at[at], f_ref.at[at], sems.at[k])
        store.start()
        stores.append(store)
    for store in stores:
        store.wait()


def fold(parts):
    return pl.pallas_call(
        fold_kernel,
        in_specs=[IN_VMEM] * (2 * len(LINES)),
        out_specs=[ANYWHERE, IN_VMEM],
        out_shape=[pltpu.HBM((PORTS, PORTS), BF16), pltpu.VMEM((DROWS, PORTS), F32)],
        scratch_shapes=[
            pltpu.VMEM((3, PORTS, PORTS), BF16),
            pltpu.VMEM((32, DROWS, PORTS), BF16),
            pltpu.VMEM((PORTS, PORTS), BF16),
            pltpu.VMEM((PORTS, PORTS), BF16),
            pltpu.SemaphoreType.DMA((4,)),
        ],
        compiler_params=params(24),
        cost_estimate=cost(14 * PORTS**3, 9 << 20),
        name="fold",
    )(*[vmem(part) for part in parts])


def finish_kernel(target_ref, ret_ref, f_ref, diag_ref, out_ref, route, response, scaled, coupling, made, in_sem, out_sems):
    load = pltpu.make_async_copy(f_ref, coupling, in_sem)
    load.start()
    code = jnp.transpose(jnp.broadcast_to(target_ref[...], (128, ROWS)))
    scale = jnp.where(code >= SLOTS, 1.0 / HALF_SCALE, 1.0)
    target = code & (SLOTS - 1)
    for j in range(0, SLOTS, 128):
        route[:, j : j + 128] = jnp.where(iota((ROWS, 128), 1) + j == target, scale, 0.0).astype(BF16)
    for n in range(0, PORTS, 256):
        at = slice(n, n + 256)
        piece = jnp.dot(route[...], ret_ref[:, at], preferred_element_type=F32)
        response[:, at] = piece
        scaled[:, at] = (piece * diag_ref[0:1, at]).astype(BF16)
    load.wait()
    stores = []
    tile = 256
    for k, n in enumerate(range(0, PORTS, tile)):
        at = slice(n, n + tile)
        coupled = lax.dot_general(
            scaled[...], coupling[at, :], (((1,), (1,)), ((), ())), preferred_element_type=F32
        )
        made[:, at] = response[:, at] * diag_ref[1:2, at] - coupled
        store = pltpu.make_async_copy(made.at[:, at], out_ref.at[:, at], out_sems.at[k])
        store.start()
        stores.append(store)
    for store in stores:
        store.wait()


def finish(target, returned, f, diag):
    return pl.pallas_call(
        finish_kernel,
        in_specs=[IN_VMEM, IN_VMEM, ANYWHERE, IN_VMEM],
        out_specs=ANYWHERE,
        out_shape=pltpu.HBM((ROWS, PORTS), F32),
        scratch_shapes=[
            pltpu.VMEM((ROWS, SLOTS), BF16),
            pltpu.VMEM((ROWS, PORTS), F32),
            pltpu.VMEM((ROWS, PORTS), BF16),
            pltpu.VMEM((PORTS, PORTS), BF16),
            pltpu.VMEM((ROWS, PORTS), F32),
            pltpu.SemaphoreType.DMA,
            pltpu.SemaphoreType.DMA((4,)),
        ],
        compiler_params=params(24),
        cost_estimate=cost(4 * ROWS * PORTS * PORTS, 6 << 20),
        name="finish",
    )(vmem(target), vmem(returned), hbm(f), vmem(diag))


def group_swap(value, mask):
    return lax.ppermute(value, "group", [(i, i ^ mask) for i in range(8)])


def chip_shift(value, step, turn):
    pairs = []
    for o in range(OWNERS):
        c, x, y = o & 1, (o >> 1) & 3, o >> 3
        if (c ^ turn) == 0:
            x = (x + step) % 4
        else:
            y = (y + step) % 4
        pairs.append((o, (y * 4 + x) * 2 + c))
    return lax.ppermute(value, "owner", pairs)


def core_swap(value):
    return lax.ppermute(value, "owner", [(o, o ^ 1) for o in range(OWNERS)])


def exchange(value):
    shape = value.shape
    value = value.reshape(OWNERS, CAP, PORTS)
    return lax.all_to_all(value, "owner", split_axis=0, concat_axis=0, tiled=True).reshape(shape)


def body(port_rows, defect_owner, defect_half, defect_port, subcircuit_maps, schur_off, schur_diag, pivot_order):
    z0 = label(schur_off, schur_diag.reshape(1, OWN))
    z1, z2, z3 = (group_swap(z0, mask) for mask in (1, 2, 3))
    outgoing, target = prep(
        defect_owner.reshape(1, ROWS), defect_half.reshape(1, ROWS), defect_port.reshape(1, ROWS), port_rows
    )
    arrived = exchange(outgoing)
    z, off, diag, gb = low_levels(z0, z1, z2, z3, pivot_order)
    pack = top_level(group_swap(z, 4), off, diag, gb, pivot_order)
    line = jnp.stack([pack] + [chip_shift(pack, step, 0) for step in STEPS])
    left, right = chip_shift(line, 1, 1), chip_shift(line, -1, 1)
    answers = apply_maps(arrived, subcircuit_maps)
    answers, left, right = lax.optimization_barrier((answers, left, right))
    far_low, far_high = chip_shift(left[:2], 1, 1), chip_shift(right[2:], -1, 1)
    parts = [line, left, right, far_low, far_high]
    parts = parts + [core_swap(part) for part in parts]
    f, inverses = fold(parts)
    returned = exchange(answers)
    return finish(target, returned, f, inverses)


def solution(mesh):
    return jax.shard_map(
        body,
        mesh=mesh,
        in_specs=(
            P(("group", "owner"), None),
            P(("group", "owner"), None),
            P(("group", "owner")),
            P(("group", "owner")),
            P(("group", "owner"), None, None),
            P(("group", "owner"), None),
            P(("group", "owner")),
            P(),
        ),
        out_specs=P(("group", "owner"), None),
        check_vma=False,
    )
```
